512 devices in a mesh: week: 32 (over z_hi, y, core), markov: 16 (over x, z_lo).
Axes of the slice: x: 4, y: 8, z: 8 (z_hi: 2, z_lo: 4; z = z_hi * 4 + z_lo), core: 2. Of those that a mesh axis runs over, the one named last changes fastest.
Arguments:
- trial_states: float32 [32, 16, 32, 2048], P('week', 'markov'), may hold values from -6 to 6
- successor: int32 [32, 16, 32, 1], P('week', 'markov'), may hold values from 0 to 15; in each aligned block of 32 rows (0 to 31, 32 to 63, ..., all dimensions but the last counted through in order) at most 4 rows name the same one
- inflow: float32 [32, 16, 2048], P('week', 'markov'), may hold values from -6 to 6
- unit_cost: float32 [32, 16, 2048], P('week', 'markov'), may hold values from -3 to 3
- curvature: float32 [32, 16, 2048], P('week', 'markov'), may hold values from 0.5 to 8
- target: float32 [32, 16, 2048], P('week', 'markov'), may hold values from -6 to 6
- release_cap: float32 [32, 16, 2048], P('week', 'markov'), may hold values from 0.3 to 3
- block_values: float32 [32, 16, 16, 2, 128, 128], P('week', 'markov'), may hold values from -0.1875 to 0.1875
- block_cols: int32 [32, 16, 16, 2], P('week', 'markov'), may hold values from 0 to 15
Outputs:
- cut_slope: float32 [32, 16, 32, 2048], P('week', 'markov')
- cut_intercept: float32 [32, 16, 32], P('week', 'markov')
The draws below stay inside these ranges and needn't reach their ends.
Inputs may be any that keep to these rules, and one draw needn't show every extreme that they name: Among the 32 rows of one node, at most 4 name the same successor state, and in every draw some node has exactly 4 rows naming one state.
All inputs are finite; a program needn't handle non-finite values.
Results may differ from the reference program's by a relative error of at most 0.0003.
Values sent between devices are 32-bit elements; how exact they have to be, the bound alone decides.
No kernel may reach another device: no remote copies, remote signals or barrier semaphores. Data moves between devices by JAX's collectives and lax.ppermute only.
A program may use at most 64 MiB of HBM per device.

```python
import math
import jax
import jax.numpy as jnp
import numpy as np
from jax import lax

R = 2048
BS = 128
KB = 2
TR = 32
ITERS = 4
NBLK = 16
WEEKS = 32
MARKOV = 16
CAP = 4


def touch_ends(array, rng, low, largest):
    spot = [jax.random.randint(jax.random.fold_in(rng, axis), (), 0, length) for axis, length in enumerate(array.shape)]
    widest = array.shape.index(max(array.shape))
    beside = spot[:widest] + [(spot[widest] + 1) % array.shape[widest]] + spot[widest + 1:]
    return array.at[tuple(spot)].set(low).at[tuple(beside)].set(largest)


def block_scale(rng, dims, shards, smallest, high):
    gain, own = 1.0, jax.random.fold_in(rng, 6)
    for position, parts in shards:
        draws = jnp.exp(jax.random.uniform(jax.random.fold_in(own, position), (parts,), jnp.float32, smallest / len(shards), high / len(shards)))
        gain = gain * jnp.repeat(draws, dims[position] // parts).reshape([-1 if axis == position else 1 for axis in range(len(dims))])
    return gain


def routed_block(own_key, own, number, rows, amount, top, bound, lean):
    sequence = jax.random.permutation(own_key, amount)
    crowded, usual = load_shares(amount, rows * top, bound, lean, True), load_shares(amount, rows * top, bound, lean, False)
    places = jnp.arange(amount)

    def named(sizes, turn):
        used = int((sizes > 0).sum())
        fixed = max(1, used // 4)
        moved = fixed + (places - fixed + turn * (used - fixed)) % max(1, amount - fixed)
        return jnp.zeros((amount,), jnp.int32).at[sequence[jnp.where(places < fixed, places, moved)]].set(jnp.asarray(sizes, jnp.int32))

    sizes = jnp.where(number % 4 == 0, named(crowded, number // 4), named(usual, number - number // 4 - 1))
    mixed = jax.random.permutation(jax.random.fold_in(own, 3), amount)
    donor, taker = mixed[0:amount // 2 * 2:2], mixed[1:amount // 2 * 2:2]
    room = jnp.minimum(sizes[donor] - 1, bound - sizes[taker]) // 2
    room = jnp.where((donor == sequence[0]) | (taker == sequence[0]) | (sizes[taker] == 0), 0, jnp.maximum(room, 0))
    moved = jax.random.randint(jax.random.fold_in(own, 4), (amount // 2,), 0, 1 << 20) % (room + 1)
    sizes = sizes.at[donor].add(-moved).at[taker].add(moved)
    labels = jnp.searchsorted(jnp.cumsum(sizes), jnp.arange(rows * top), side="right").astype(jnp.int32)
    table = labels.reshape(top, rows).T
    table = table[jax.random.permutation(jax.random.fold_in(own, 1), rows)]
    turn = jax.random.randint(jax.random.fold_in(own, 2), (rows, 1), 0, top)
    return jnp.take_along_axis(table, (jnp.arange(top)[None, :] + turn) % top, axis=1)


def load_shares(amount, total, reach, slope, full):
    portions = [(1 << 20) // math.isqrt(standing ** slope) + 1 for standing in range(1, amount + 1)]
    largest = reach if full else min(reach, max(-(-total // amount), total * portions[0] // sum(portions)))
    least = 1 if total - largest >= amount - 1 else 0
    given, spare = [largest] + [least] * (amount - 1), total - largest - least * (amount - 1)
    while spare > 0:
        candidates = [i for i in range(1, amount) if given[i] < largest] or [i for i in range(1, amount) if given[i] < reach]
        mass, remaining = sum([portions[i] for i in candidates]), spare
        for i in candidates:
            addition = min(reach - given[i], max(1, remaining * portions[i] // mass), spare)
            given[i] = given[i] + addition
            spare = spare - addition
    return np.array(given)


def gaussian(key, dims, scale, limit, cuts=(), kind=jnp.bfloat16):
    loudness = block_scale(key, dims, cuts, -0.22, 0.18) if cuts else 1.0
    result = jax.random.normal(key, dims, jnp.float32) * scale * loudness
    return jnp.minimum(jnp.maximum(result, -limit), limit).astype(kind)


def setup_inputs(seed: int = 0) -> dict:
    streams_of = jax.random.split(jax.random.key(seed), 10)
    trial_states = gaussian(streams_of[0], (WEEKS, MARKOV, TR, R), 1.0, 6.0, ((0, 32), (1, 16)), jnp.float32)
    successor_keys = jax.random.split(jax.random.fold_in(streams_of[1], 1), WEEKS * MARKOV * TR // TR)
    successor_turns = jax.random.permutation(jax.random.fold_in(streams_of[1], 3), WEEKS * MARKOV * TR // TR)
    successor = jax.vmap(lambda own, number: routed_block(jax.random.fold_in(streams_of[1], 2), own, number, TR, MARKOV, 1, CAP, 2))(successor_keys, successor_turns).reshape((WEEKS, MARKOV, TR, 1))
    inflow = gaussian(streams_of[2], (WEEKS, MARKOV, R), 1.0, 6.0, ((0, 32), (1, 16)), jnp.float32)
    unit_cost = gaussian(streams_of[3], (WEEKS, MARKOV, R), 0.5, 3.0, ((0, 32), (1, 16)), jnp.float32)
    curvature = jnp.clip(jnp.exp(math.log(8.0) - 2.7725887 * jax.random.uniform(streams_of[4], (WEEKS, MARKOV, R), jnp.float32) ** block_scale(streams_of[4], (WEEKS, MARKOV, R), ((0, 32), (1, 16)), -0.2, 0.2)), 0.5, 8.0)
    target = gaussian(streams_of[5], (WEEKS, MARKOV, R), 1.0, 6.0, ((0, 32), (1, 16)), jnp.float32)
    release_cap = jnp.clip(jnp.exp(math.log(3.0) - 2.3025851 * jax.random.uniform(streams_of[6], (WEEKS, MARKOV, R), jnp.float32) ** block_scale(streams_of[6], (WEEKS, MARKOV, R), ((0, 32), (1, 16)), -0.2, 0.2)), 0.3, 3.0)
    block_values = gaussian(streams_of[7], (WEEKS, MARKOV, NBLK, KB, BS, BS), (4 * KB * BS) ** -0.5, 0.1875, ((0, 32), (1, 16)), jnp.float32)
    block_cols = touch_ends(jax.random.randint(streams_of[8], (WEEKS, MARKOV, NBLK, KB), 0, NBLK), jax.random.fold_in(streams_of[8], 1), 0, NBLK - 1).astype(jnp.int32)
    return dict(trial_states=trial_states, successor=successor, inflow=inflow, unit_cost=unit_cost, curvature=curvature, target=target, release_cap=release_cap, block_values=block_values, block_cols=block_cols)


highest = lax.Precision.HIGHEST
dual_step = 0.5
primal_step = 0.5


def slot_matrix(dest_row, states, capacity):
    marked = (dest_row[:, None] == jnp.arange(states, dtype=jnp.int32)[None, :]).astype(jnp.int32)
    ranked = jnp.sum(jnp.cumsum(marked, axis=0) * marked, axis=1) - 1
    slot_ids = dest_row * capacity + ranked
    return (slot_ids[None, :] == jnp.arange(states * capacity, dtype=jnp.int32)[:, None]).astype(jnp.float32)


def solve_rows(rows, inflow, unit_cost, curvature, target, release_cap, block_values, block_cols):
    count, width = rows.shape
    nblk, kblk, bsize = block_values.shape[0], block_values.shape[1], block_values.shape[2]
    picker = (block_cols[:, :, None] == jnp.arange(nblk, dtype=jnp.int32)[None, None, :]).astype(jnp.float32)

    def apply_fwd(field):
        split = field.reshape(count, nblk, bsize)
        taken = jnp.einsum('rjb,nkj->rnkb', split, picker, precision=highest)
        mixed = jnp.einsum('rnkb,nkcb->rnc', taken, block_values, precision=highest)
        return field + mixed.reshape(count, width)

    def apply_adj(field):
        split = field.reshape(count, nblk, bsize)
        spread = jnp.einsum('rnc,nkcb->rnkb', split, block_values, precision=highest)
        summed = jnp.einsum('rnkb,nkj->rjb', spread, picker, precision=highest)
        return field + summed.reshape(count, width)

    base = rows + inflow[None, :] - target[None, :]
    shrink = curvature / (curvature + dual_step)
    release = jnp.zeros((count, width), jnp.float32)
    extrap = jnp.zeros((count, width), jnp.float32)
    dual = jnp.zeros((count, width), jnp.float32)
    for sweep_index in range(ITERS):
        dual = (dual + dual_step * (base - apply_fwd(extrap))) * shrink[None, :]
        fresh = jnp.clip(release + primal_step * (apply_adj(dual) - unit_cost[None, :]), 0.0, release_cap[None, :])
        extrap = 2.0 * fresh - release
        release = fresh
    storage = rows + inflow[None, :] - apply_fwd(release)
    gap = storage - target[None, :]
    value = jnp.mean(unit_cost[None, :] * release + 0.5 * curvature[None, :] * gap * gap, axis=1)
    icpt = value - jnp.mean(dual * rows, axis=1)
    return dual, icpt


def reference(trial_states, successor, inflow, unit_cost, curvature, target, release_cap, block_values, block_cols):
    def one_week(week):
        source = (week - 1 + WEEKS) % WEEKS
        rows = lax.dynamic_index_in_dim(trial_states, source, 0, keepdims=False)
        dests = lax.dynamic_index_in_dim(successor, source, 0, keepdims=False)[:, :, 0]
        placers = jax.vmap(lambda dest_row: slot_matrix(dest_row, MARKOV, CAP))(dests)
        packed = jnp.einsum('sqt,str->sqr', placers, rows, precision=highest)
        packed = packed.reshape(MARKOV, MARKOV, CAP, R).transpose(1, 0, 2, 3).reshape(MARKOV, MARKOV * CAP, R)
        node_data = tuple(lax.dynamic_index_in_dim(arr, week, 0, keepdims=False)
                          for arr in (inflow, unit_cost, curvature, target, release_cap, block_values, block_cols))

        def one_node(items):
            return solve_rows(*items)

        slopes, icpts = lax.map(one_node, (packed,) + node_data)
        slopes = slopes.reshape(MARKOV, MARKOV, CAP, R).transpose(1, 0, 2, 3).reshape(MARKOV, MARKOV * CAP, R)
        icpts = icpts.reshape(MARKOV, MARKOV, CAP).transpose(1, 0, 2).reshape(MARKOV, MARKOV * CAP)
        mine = jnp.einsum('sqt,sqr->str', placers, slopes, precision=highest)
        mine_icpt = jnp.einsum('sqt,sq->st', placers, icpts, precision=highest)
        return mine, mine_icpt

    slopes_all, icpts_all = lax.map(one_week, jnp.arange(WEEKS, dtype=jnp.int32))
    return jnp.roll(slopes_all, -1, axis=0), jnp.roll(icpts_all, -1, axis=0)
```

```python
import functools

import jax
import jax.numpy as jnp
from jax import lax
from jax.experimental import pallas as pl
from jax.experimental.pallas import tpu as pltpu
from jax.sharding import PartitionSpec as P

ITERS = 4
BS = 128

highest = lax.Precision.HIGHEST
dual_step = 0.5
primal_step = 0.5


def shifted(value, axis, steps):
    count = lax.axis_size(axis)
    pairs = [(source, (source + steps) % count) for source in range(count)]
    return lax.ppermute(value, axis, pairs)


def mat_nt(a, b):
    return lax.dot_general(a, b, (((1,), (1,)), ((), ())), precision=highest,
                           preferred_element_type=jnp.float32)


def mat_nn(a, b):
    return lax.dot_general(a, b, (((1,), (0,)), ((), ())), precision=highest,
                           preferred_element_type=jnp.float32)


def solve_kernel(nblk, kblk, cols_ref, rows_ref, xi_ref, c_ref, q_ref, g_ref, h_ref, bv_ref,
                 out_ref, base_s, p_s, u_s, v_s, acc_s):
    width = nblk * BS

    def lanes(n):
        return slice(n * BS, (n + 1) * BS)

    def col(n, k):
        return cols_ref[n * kblk + k]

    def apply_fwd(field_s, n):
        total = field_s[n]
        for k in range(kblk):
            total = total + mat_nt(field_s[col(n, k)], bv_ref[n, k])
        return total

    for n in range(nblk):
        s = lanes(n)
        base_s[n] = rows_ref[:, s] + xi_ref[:, s] - g_ref[:, s]
        u_s[n] = jnp.zeros(u_s.shape[1:], jnp.float32)

    for sweep in range(ITERS):
        for n in range(nblk):
            s = lanes(n)
            q = q_ref[:, s]
            shrink = q / (q + dual_step)
            if sweep == 0:
                p_s[n] = (dual_step * base_s[n]) * shrink
            else:
                p_s[n] = (p_s[n] + dual_step * (base_s[n] - apply_fwd(v_s, n))) * shrink
        for n in range(nblk):
            acc_s[n] = jnp.zeros(acc_s.shape[1:], jnp.float32)
        for n in range(nblk):
            pn = p_s[n]
            for k in range(kblk):
                c = col(n, k)
                acc_s[c] = acc_s[c] + mat_nn(pn, bv_ref[n, k])
        for n in range(nblk):
            s = lanes(n)
            u_old = u_s[n]
            fresh = jnp.clip(u_old + primal_step * (p_s[n] + acc_s[n] - c_ref[:, s]), 0.0, h_ref[:, s])
            v_s[n] = 2.0 * fresh - u_old
            u_s[n] = fresh

    value = jnp.zeros((rows_ref.shape[0], 1), jnp.float32)
    cross = jnp.zeros((rows_ref.shape[0], 1), jnp.float32)
    for n in range(nblk):
        s = lanes(n)
        rows = rows_ref[:, s]
        un = u_s[n]
        gap = rows + xi_ref[:, s] - apply_fwd(u_s, n) - g_ref[:, s]
        term = c_ref[:, s] * un + 0.5 * q_ref[:, s] * gap * gap
        value = value + jnp.sum(term, axis=1, keepdims=True)
        pn = p_s[n]
        cross = cross + jnp.sum(pn * rows, axis=1, keepdims=True)
        out_ref[:, s] = pn
    icpt = (value - cross) / width
    out_ref[:, width:] = jnp.broadcast_to(icpt, (rows_ref.shape[0], BS))


def solve_block(rows, inflow, unit_cost, curvature, target, release_cap, block_values, block_cols):
    count, width = rows.shape
    nblk, kblk = block_values.shape[0], block_values.shape[1]
    vec = lambda a: a.reshape(1, width)
    vspec = pl.BlockSpec(memory_space=pltpu.VMEM)
    field = pltpu.VMEM((nblk, count, BS), jnp.float32)
    flops = 2 * count * nblk * kblk * BS * BS * (2 * ITERS + 1) * 6
    return pl.pallas_call(
        functools.partial(solve_kernel, nblk, kblk),
        out_shape=jax.ShapeDtypeStruct((count, width + BS), jnp.float32),
        in_specs=[pl.BlockSpec(memory_space=pltpu.SMEM)] + [vspec] * 7,
        out_specs=vspec,
        scratch_shapes=[field] * 5,
        compiler_params=pltpu.CompilerParams(vmem_limit_bytes=48 * 1024 * 1024),
        cost_estimate=pl.CostEstimate(flops=flops, transcendentals=0,
                                      bytes_accessed=4 * (block_values.size + 3 * rows.size)),
        name="sddp_solve",
    )(block_cols.reshape(-1), rows, vec(inflow), vec(unit_cost), vec(curvature), vec(target),
      vec(release_cap), block_values)


def on_device(trial_states, successor, inflow, unit_cost, curvature, target, release_cap,
              block_values, block_cols):
    states = lax.axis_size("markov")
    tr_rows = trial_states.shape[2]
    width = trial_states.shape[3]
    capacity = 2 * tr_rows // states
    slots = states * capacity
    own_rows = trial_states.reshape(tr_rows, width)
    own_dest = successor.reshape(tr_rows)
    rows, dest = shifted((own_rows, own_dest), "week", 1)
    marked = (dest[:, None] == jnp.arange(states, dtype=jnp.int32)[None, :]).astype(jnp.int32)
    ranked = jnp.sum(jnp.cumsum(marked, axis=0) * marked, axis=1) - 1
    slot_ids = dest * capacity + ranked
    hit = slot_ids[None, :] == jnp.arange(slots, dtype=jnp.int32)[:, None]
    source = jnp.sum(jnp.where(hit, jnp.arange(tr_rows, dtype=jnp.int32)[None, :], 0), axis=1)
    filled = jnp.any(hit, axis=1)
    packed = jnp.where(filled[:, None], jnp.take(rows, source, axis=0), 0.0)
    arrived = lax.all_to_all(packed.reshape(states, capacity, width), "markov", 0, 0, tiled=True)
    solved = solve_block(arrived.reshape(slots, width), inflow.reshape(width),
                         unit_cost.reshape(width), curvature.reshape(width), target.reshape(width),
                         release_cap.reshape(width), block_values[0, 0], block_cols[0, 0])
    back = lax.all_to_all(solved.reshape(states, capacity, -1), "markov", 0, 0, tiled=True)
    mine = jnp.take(back.reshape(slots, -1), slot_ids, axis=0)
    mine = shifted(mine, "week", -1)
    return (mine[:, :width].reshape(1, 1, tr_rows, width),
            mine[:, width].reshape(1, 1, tr_rows))


def solution(mesh):
    return jax.shard_map(
        on_device,
        mesh=mesh,
        in_specs=(
            P("week", "markov", None, None),
            P("week", "markov", None, None),
            P("week", "markov", None),
            P("week", "markov", None),
            P("week", "markov", None),
            P("week", "markov", None),
            P("week", "markov", None),
            P("week", "markov", None, None, None, None),
            P("week", "markov", None, None),
        ),
        out_specs=(P("week", "markov", None, None), P("week", "markov", None)),
        check_vma=False,
    )
```

```python
import functools

import jax
import jax.numpy as jnp
from jax import lax
from jax.experimental import pallas as pl
from jax.experimental.pallas import tpu as pltpu
from jax.sharding import PartitionSpec as P

ITERS = 4
BS = 128

dual_step = 0.5
primal_step = 0.5


def shifted(value, axis, steps):
    count = lax.axis_size(axis)
    pairs = [(source, (source + steps) % count) for source in range(count)]
    return lax.ppermute(value, axis, pairs)


def dotb(a, b):
    return lax.dot_general(a, b, (((1,), (0,)), ((), ())), preferred_element_type=jnp.float32)


def split(x):
    hi = x.astype(jnp.bfloat16)
    return hi, (x - hi.astype(jnp.float32)).astype(jnp.bfloat16)


def mm(x, wh, wl):
    xh, xl = split(x)
    return dotb(xh, wh) + dotb(xl, wh) + dotb(xh, wl)


def solve_kernel(nblk, kblk, cols_ref, rows_ref, xi_ref, c_ref, q_ref, g_ref, h_ref, bv_ref,
                 out_ref, base_s, p_s, u_s, v_s, acc_s, fh, fl, ah, al):
    width = nblk * BS
    rows_n = rows_ref.shape[0]

    def lanes(n):
        return slice(n * BS, (n + 1) * BS)

    def col(n, k):
        return cols_ref[n * kblk + k]

    for n in range(nblk):
        hi, lo = split(jnp.concatenate([bv_ref[n, k].T for k in range(kblk)], axis=0))
        fh[n] = hi
        fl[n] = lo
        hi, lo = split(jnp.concatenate([bv_ref[n, k] for k in range(kblk)], axis=1))
        ah[n] = hi
        al[n] = lo

    def mixed_fwd(field_s, n):
        x = jnp.concatenate([field_s[col(n, k)] for k in range(kblk)], axis=1)
        return mm(x, fh[n], fl[n])

    for n in range(nblk):
        s = lanes(n)
        base_s[n] = rows_ref[:, s] + xi_ref[:, s] - g_ref[:, s]
        u_s[n] = jnp.zeros(u_s.shape[1:], jnp.float32)

    for sweep in range(ITERS):
        for n in range(nblk):
            s = lanes(n)
            q = q_ref[:, s]
            shrink = q / (q + dual_step)
            if sweep == 0:
                p_s[n] = (dual_step * base_s[n]) * shrink
            else:
                av = v_s[n] + mixed_fwd(v_s, n)
                p_s[n] = (p_s[n] + dual_step * (base_s[n] - av)) * shrink
        for n in range(nblk):
            acc_s[n] = jnp.zeros(acc_s.shape[1:], jnp.float32)
        for n in range(nblk):
            r = mm(p_s[n], ah[n], al[n])
            for k in range(kblk):
                c = col(n, k)
                acc_s[c] = acc_s[c] + r[:, k * BS:(k + 1) * BS]
        for n in range(nblk):
            s = lanes(n)
            u_old = u_s[n]
            fresh = jnp.clip(u_old + primal_step * (p_s[n] + acc_s[n] - c_ref[:, s]), 0.0, h_ref[:, s])
            v_s[n] = 2.0 * fresh - u_old
            u_s[n] = fresh

    value = jnp.zeros((rows_n, 1), jnp.float32)
    cross = jnp.zeros((rows_n, 1), jnp.float32)
    for n in range(nblk):
        s = lanes(n)
        rows = rows_ref[:, s]
        un = u_s[n]
        gap = rows + xi_ref[:, s] - (un + mixed_fwd(u_s, n)) - g_ref[:, s]
        term = c_ref[:, s] * un + 0.5 * q_ref[:, s] * gap * gap
        value = value + jnp.sum(term, axis=1, keepdims=True)
        pn = p_s[n]
        cross = cross + jnp.sum(pn * rows, axis=1, keepdims=True)
        out_ref[:, s] = pn
    icpt = (value - cross) / width
    out_ref[:, width:] = jnp.broadcast_to(icpt, (rows_n, BS))


def solve_block(rows, inflow, unit_cost, curvature, target, release_cap, block_values, block_cols):
    count, width = rows.shape
    nblk, kblk = block_values.shape[0], block_values.shape[1]
    vec = lambda a: a.reshape(1, width)
    vspec = pl.BlockSpec(memory_space=pltpu.VMEM)
    field = pltpu.VMEM((nblk, count, BS), jnp.float32)
    scratch = [field] * 5
    scratch += [pltpu.VMEM((nblk, kblk * BS, BS), jnp.bfloat16)] * 2
    scratch += [pltpu.VMEM((nblk, BS, kblk * BS), jnp.bfloat16)] * 2
    flops = 2 * count * nblk * kblk * BS * BS * (2 * ITERS) * 3
    return pl.pallas_call(
        functools.partial(solve_kernel, nblk, kblk),
        out_shape=jax.ShapeDtypeStruct((count, width + BS), jnp.float32),
        in_specs=[pl.BlockSpec(memory_space=pltpu.SMEM)] + [vspec] * 7,
        out_specs=vspec,
        scratch_shapes=scratch,
        compiler_params=pltpu.CompilerParams(vmem_limit_bytes=48 * 1024 * 1024),
        cost_estimate=pl.CostEstimate(flops=flops, transcendentals=0,
                                      bytes_accessed=4 * (block_values.size + 3 * rows.size)),
        name="sddp_solve",
    )(block_cols.reshape(-1), rows, vec(inflow), vec(unit_cost), vec(curvature), vec(target),
      vec(release_cap), block_values)


def on_device(trial_states, successor, inflow, unit_cost, curvature, target, release_cap,
              block_values, block_cols):
    states = lax.axis_size("markov")
    tr_rows = trial_states.shape[2]
    width = trial_states.shape[3]
    capacity = 2 * tr_rows // states
    slots = states * capacity
    own_rows = trial_states.reshape(tr_rows, width)
    own_dest = successor.reshape(tr_rows)
    tag = jnp.broadcast_to(own_dest.astype(jnp.float32)[:, None], (tr_rows, BS))
    sent = shifted(jnp.concatenate([own_rows, tag], axis=1), "week", 1)
    rows, dest = sent[:, :width], sent[:, width].astype(jnp.int32)
    marked = (dest[:, None] == jnp.arange(states, dtype=jnp.int32)[None, :]).astype(jnp.int32)
    ranked = jnp.sum(jnp.cumsum(marked, axis=0) * marked, axis=1) - 1
    slot_ids = dest * capacity + ranked
    hit = slot_ids[None, :] == jnp.arange(slots, dtype=jnp.int32)[:, None]
    source = jnp.sum(jnp.where(hit, jnp.arange(tr_rows, dtype=jnp.int32)[None, :], 0), axis=1)
    filled = jnp.any(hit, axis=1)
    packed = jnp.where(filled[:, None], jnp.take(rows, source, axis=0), 0.0)
    arrived = lax.all_to_all(packed.reshape(states, capacity, width), "markov", 0, 0, tiled=True)
    solved = solve_block(arrived.reshape(slots, width), inflow.reshape(width),
                         unit_cost.reshape(width), curvature.reshape(width), target.reshape(width),
                         release_cap.reshape(width), block_values[0, 0], block_cols[0, 0])
    back = lax.all_to_all(solved.reshape(states, capacity, -1), "markov", 0, 0, tiled=True)
    mine = jnp.take(back.reshape(slots, -1), slot_ids, axis=0)
    mine = shifted(mine, "week", -1)
    return (mine[:, :width].reshape(1, 1, tr_rows, width),
            mine[:, width].reshape(1, 1, tr_rows))


def solution(mesh):
    return jax.shard_map(
        on_device,
        mesh=mesh,
        in_specs=(
            P("week", "markov", None, None),
            P("week", "markov", None, None),
            P("week", "markov", None),
            P("week", "markov", None),
            P("week", "markov", None),
            P("week", "markov", None),
            P("week", "markov", None),
            P("week", "markov", None, None, None, None),
            P("week", "markov", None, None),
        ),
        out_specs=(P("week", "markov", None, None), P("week", "markov", None)),
        check_vma=False,
    )
```

```python
import functools

import jax
import jax.numpy as jnp
from jax import lax
from jax.experimental import pallas as pl
from jax.experimental.pallas import tpu as pltpu
from jax.sharding import PartitionSpec as P

ITERS = 4
BS = 128

dual_step = 0.5
primal_step = 0.5


def shifted(value, axis, steps):
    count = lax.axis_size(axis)
    pairs = [(source, (source + steps) % count) for source in range(count)]
    return lax.ppermute(value, axis, pairs)


def dotb(a, b):
    return lax.dot_general(a, b, (((1,), (0,)), ((), ())), preferred_element_type=jnp.float32)


def split(x):
    hi = x.astype(jnp.bfloat16)
    return hi, (x - hi.astype(jnp.float32)).astype(jnp.bfloat16)


def mm(x, wh, wl):
    xh, xl = split(x)
    return dotb(xh, wh) + dotb(xl, wh) + dotb(xh, wl)


def split_kernel(nblk, kblk, bv_ref, fh, fl, ah, al):
    for n in range(nblk):
        hi, lo = split(jnp.concatenate([bv_ref[n, k].T for k in range(kblk)], axis=0))
        fh[n] = hi
        fl[n] = lo
        hi, lo = split(jnp.concatenate([bv_ref[n, k] for k in range(kblk)], axis=1))
        ah[n] = hi
        al[n] = lo


def split_blocks(block_values):
    nblk, kblk = block_values.shape[0], block_values.shape[1]
    vspec = pl.BlockSpec(memory_space=pltpu.VMEM)
    fwd = jax.ShapeDtypeStruct((nblk, kblk * BS, BS), jnp.bfloat16)
    adj = jax.ShapeDtypeStruct((nblk, BS, kblk * BS), jnp.bfloat16)
    return pl.pallas_call(
        functools.partial(split_kernel, nblk, kblk),
        out_shape=(fwd, fwd, adj, adj),
        in_specs=[vspec],
        out_specs=(vspec,) * 4,
        cost_estimate=pl.CostEstimate(flops=4 * block_values.size, transcendentals=0,
                                      bytes_accessed=8 * block_values.size),
        name="sddp_split",
    )(block_values)


def solve_kernel(nblk, kblk, cols_ref, rows_ref, xi_ref, c_ref, q_ref, g_ref, h_ref,
                 fh, fl, ah, al, out_ref, base_s, p_s, u_s, v_s, acc_s):
    width = nblk * BS
    rows_n = rows_ref.shape[0]

    def lanes(n):
        return slice(n * BS, (n + 1) * BS)

    def col(n, k):
        return cols_ref[n * kblk + k]

    def mixed_fwd(field_s, n):
        x = jnp.concatenate([field_s[col(n, k)] for k in range(kblk)], axis=1)
        return mm(x, fh[n], fl[n])

    for n in range(nblk):
        s = lanes(n)
        base_s[n] = rows_ref[:, s] + xi_ref[:, s] - g_ref[:, s]
        u_s[n] = jnp.zeros(u_s.shape[1:], jnp.float32)

    for sweep in range(ITERS):
        for n in range(nblk):
            s = lanes(n)
            q = q_ref[:, s]
            shrink = q / (q + dual_step)
            if sweep == 0:
                p_s[n] = (dual_step * base_s[n]) * shrink
            else:
                av = v_s[n] + mixed_fwd(v_s, n)
                p_s[n] = (p_s[n] + dual_step * (base_s[n] - av)) * shrink
        for n in range(nblk):
            acc_s[n] = jnp.zeros(acc_s.shape[1:], jnp.float32)
        for n in range(nblk):
            r = mm(p_s[n], ah[n], al[n])
            for k in range(kblk):
                c = col(n, k)
                acc_s[c] = acc_s[c] + r[:, k * BS:(k + 1) * BS]
        for n in range(nblk):
            s = lanes(n)
            u_old = u_s[n]
            fresh = jnp.clip(u_old + primal_step * (p_s[n] + acc_s[n] - c_ref[:, s]), 0.0, h_ref[:, s])
            v_s[n] = 2.0 * fresh - u_old
            u_s[n] = fresh

    value = jnp.zeros((rows_n, 1), jnp.float32)
    cross = jnp.zeros((rows_n, 1), jnp.float32)
    for n in range(nblk):
        s = lanes(n)
        rows = rows_ref[:, s]
        un = u_s[n]
        gap = rows + xi_ref[:, s] - (un + mixed_fwd(u_s, n)) - g_ref[:, s]
        term = c_ref[:, s] * un + 0.5 * q_ref[:, s] * gap * gap
        value = value + jnp.sum(term, axis=1, keepdims=True)
        pn = p_s[n]
        cross = cross + jnp.sum(pn * rows, axis=1, keepdims=True)
        out_ref[:, s] = pn
    icpt = (value - cross) / width
    out_ref[:, width:] = jnp.broadcast_to(icpt, (rows_n, BS))


def solve_block(rows, inflow, unit_cost, curvature, target, release_cap, block_values, block_cols):
    count, width = rows.shape
    nblk, kblk = block_values.shape[0], block_values.shape[1]
    vec = lambda a: a.reshape(1, width)
    vspec = pl.BlockSpec(memory_space=pltpu.VMEM)
    field = pltpu.VMEM((nblk, count, BS), jnp.float32)
    flops = 2 * count * nblk * kblk * BS * BS * (2 * ITERS) * 3
    return pl.pallas_call(
        functools.partial(solve_kernel, nblk, kblk),
        out_shape=jax.ShapeDtypeStruct((count, width + BS), jnp.float32),
        in_specs=[pl.BlockSpec(memory_space=pltpu.SMEM)] + [vspec] * 10,
        out_specs=vspec,
        scratch_shapes=[field] * 5,
        compiler_params=pltpu.CompilerParams(vmem_limit_bytes=48 * 1024 * 1024),
        cost_estimate=pl.CostEstimate(flops=flops, transcendentals=0,
                                      bytes_accessed=4 * (block_values.size + 3 * rows.size)),
        name="sddp_solve",
    )(block_cols.reshape(-1), rows, vec(inflow), vec(unit_cost), vec(curvature), vec(target),
      vec(release_cap), *split_blocks(block_values))


def on_device(trial_states, successor, inflow, unit_cost, curvature, target, release_cap,
              block_values, block_cols):
    states = lax.axis_size("markov")
    tr_rows = trial_states.shape[2]
    width = trial_states.shape[3]
    capacity = 2 * tr_rows // states
    slots = states * capacity
    own_rows = trial_states.reshape(tr_rows, width)
    own_dest = successor.reshape(tr_rows)
    tag = jnp.broadcast_to(own_dest.astype(jnp.float32)[:, None], (tr_rows, BS))
    sent = shifted(jnp.concatenate([own_rows, tag], axis=1), "week", 1)
    rows, dest = sent[:, :width], sent[:, width].astype(jnp.int32)
    marked = (dest[:, None] == jnp.arange(states, dtype=jnp.int32)[None, :]).astype(jnp.int32)
    ranked = jnp.sum(jnp.cumsum(marked, axis=0) * marked, axis=1) - 1
    slot_ids = dest * capacity + ranked
    hit = slot_ids[None, :] == jnp.arange(slots, dtype=jnp.int32)[:, None]
    source = jnp.sum(jnp.where(hit, jnp.arange(tr_rows, dtype=jnp.int32)[None, :], 0), axis=1)
    packed = jnp.take(rows, source, axis=0, mode="clip")
    arrived = lax.all_to_all(packed.reshape(states, capacity, width), "markov", 0, 0, tiled=True)
    solved = solve_block(arrived.reshape(slots, width), inflow.reshape(width),
                         unit_cost.reshape(width), curvature.reshape(width), target.reshape(width),
                         release_cap.reshape(width), block_values[0, 0], block_cols[0, 0])
    back = lax.all_to_all(solved.reshape(states, capacity, -1), "markov", 0, 0, tiled=True)
    mine = jnp.take(back.reshape(slots, -1), slot_ids, axis=0, mode="clip")
    mine = shifted(mine, "week", -1)
    return (mine[:, :width].reshape(1, 1, tr_rows, width),
            mine[:, width].reshape(1, 1, tr_rows))


def solution(mesh):
    return jax.shard_map(
        on_device,
        mesh=mesh,
        in_specs=(
            P("week", "markov", None, None),
            P("week", "markov", None, None),
            P("week", "markov", None),
            P("week", "markov", None),
            P("week", "markov", None),
            P("week", "markov", None),
            P("week", "markov", None),
            P("week", "markov", None, None, None, None),
            P("week", "markov", None, None),
        ),
        out_specs=(P("week", "markov", None, None), P("week", "markov", None)),
        check_vma=False,
    )
```

```python
import functools

import jax
import jax.numpy as jnp
from jax import lax
from jax.experimental import pallas as pl
from jax.experimental.pallas import tpu as pltpu
from jax.sharding import PartitionSpec as P

ITERS = 4
BS = 128

dual_step = 0.5
primal_step = 0.5


def shifted(value, axis, steps):
    count = lax.axis_size(axis)
    pairs = [(source, (source + steps) % count) for source in range(count)]
    return lax.ppermute(value, axis, pairs)


def dotb(a, b):
    return lax.dot_general(a, b, (((1,), (0,)), ((), ())), preferred_element_type=jnp.float32)


def split(x):
    hi = x.astype(jnp.bfloat16)
    return hi, (x - hi.astype(jnp.float32)).astype(jnp.bfloat16)


def mm(x, wh, wl):
    xh, xl = split(x)
    return dotb(xh, wh) + dotb(xl, wh) + dotb(xh, wl)


def solve_kernel(nblk, kblk, cols_ref, rows_ref, xi_ref, c_ref, q_ref, g_ref, h_ref, bv_ref,
                 out_ref, base_s, p_s, u_s, v_s, acc_s, fh, fl, ah, al):
    width = nblk * BS
    rows_n = rows_ref.shape[0]

    def lanes(n):
        return slice(n * BS, (n + 1) * BS)

    def col(n, k):
        return cols_ref[n * kblk + k]

    for n in range(nblk):
        hi, lo = split(jnp.concatenate([bv_ref[n, k].T for k in range(kblk)], axis=0))
        fh[n] = hi
        fl[n] = lo
        hi, lo = split(jnp.concatenate([bv_ref[n, k] for k in range(kblk)], axis=1))
        ah[n] = hi
        al[n] = lo

    def mixed_fwd(field_s, n):
        x = jnp.concatenate([field_s[col(n, k)] for k in range(kblk)], axis=1)
        return mm(x, fh[n], fl[n])

    for n in range(nblk):
        s = lanes(n)
        base_s[n] = rows_ref[:, s] + xi_ref[:, s] - g_ref[:, s]
        u_s[n] = jnp.zeros(u_s.shape[1:], jnp.float32)

    for sweep in range(ITERS):
        for n in range(nblk):
            s = lanes(n)
            q = q_ref[:, s]
            shrink = q / (q + dual_step)
            if sweep == 0:
                p_s[n] = (dual_step * base_s[n]) * shrink
            else:
                av = v_s[n] + mixed_fwd(v_s, n)
                p_s[n] = (p_s[n] + dual_step * (base_s[n] - av)) * shrink
        for n in range(nblk):
            acc_s[n] = jnp.zeros(acc_s.shape[1:], jnp.float32)
        for n in range(nblk):
            r = mm(p_s[n], ah[n], al[n])
            for k in range(kblk):
                c = col(n, k)
                acc_s[c] = acc_s[c] + r[:, k * BS:(k + 1) * BS]
        for n in range(nblk):
            s = lanes(n)
            u_old = u_s[n]
            fresh = jnp.clip(u_old + primal_step * (p_s[n] + acc_s[n] - c_ref[:, s]), 0.0, h_ref[:, s])
            v_s[n] = 2.0 * fresh - u_old
            u_s[n] = fresh

    value = jnp.zeros((rows_n, 1), jnp.float32)
    cross = jnp.zeros((rows_n, 1), jnp.float32)
    for n in range(nblk):
        s = lanes(n)
        rows = rows_ref[:, s]
        un = u_s[n]
        gap = rows + xi_ref[:, s] - (un + mixed_fwd(u_s, n)) - g_ref[:, s]
        term = c_ref[:, s] * un + 0.5 * q_ref[:, s] * gap * gap
        value = value + jnp.sum(term, axis=1, keepdims=True)
        pn = p_s[n]
        cross = cross + jnp.sum(pn * rows, axis=1, keepdims=True)
        out_ref[:, s] = pn
    icpt = (value - cross) / width
    out_ref[:, width:] = jnp.broadcast_to(icpt, (rows_n, BS))


def solve_block(rows, inflow, unit_cost, curvature, target, release_cap, block_values, block_cols):
    count, width = rows.shape
    nblk, kblk = block_values.shape[0], block_values.shape[1]
    vec = lambda a: a.reshape(1, width)
    vspec = pl.BlockSpec(memory_space=pltpu.VMEM)
    field = pltpu.VMEM((nblk, count, BS), jnp.float32)
    scratch = [field] * 5
    scratch += [pltpu.VMEM((nblk, kblk * BS, BS), jnp.bfloat16)] * 2
    scratch += [pltpu.VMEM((nblk, BS, kblk * BS), jnp.bfloat16)] * 2
    flops = 2 * count * nblk * kblk * BS * BS * (2 * ITERS) * 3
    return pl.pallas_call(
        functools.partial(solve_kernel, nblk, kblk),
        out_shape=jax.ShapeDtypeStruct((count, width + BS), jnp.float32),
        in_specs=[pl.BlockSpec(memory_space=pltpu.SMEM)] + [vspec] * 7,
        out_specs=vspec,
        scratch_shapes=scratch,
        compiler_params=pltpu.CompilerParams(vmem_limit_bytes=48 * 1024 * 1024),
        cost_estimate=pl.CostEstimate(flops=flops, transcendentals=0,
                                      bytes_accessed=4 * (block_values.size + 3 * rows.size)),
        name="sddp_solve",
    )(block_cols.reshape(-1), rows, vec(inflow), vec(unit_cost), vec(curvature), vec(target),
      vec(release_cap), block_values)


def on_device(trial_states, successor, inflow, unit_cost, curvature, target, release_cap,
              block_values, block_cols):
    states = lax.axis_size("markov")
    tr_rows = trial_states.shape[2]
    width = trial_states.shape[3]
    capacity = 2 * tr_rows // states
    slots = states * capacity
    nblk, kblk = block_cols.shape[2], block_cols.shape[3]
    rows = trial_states.reshape(tr_rows, width)
    dest = successor.reshape(tr_rows)
    vectors = jnp.stack([a.reshape(width) for a in (inflow, unit_cost, curvature, target, release_cap)])
    cols = jnp.zeros((1, width), jnp.float32).at[0, :nblk * kblk].set(
        block_cols.reshape(-1).astype(jnp.float32))
    node_blocks, node_small = shifted((block_values[0, 0], jnp.concatenate([vectors, cols])), "week", -1)
    marked = (dest[:, None] == jnp.arange(states, dtype=jnp.int32)[None, :]).astype(jnp.int32)
    ranked = jnp.sum(jnp.cumsum(marked, axis=0) * marked, axis=1) - 1
    slot_ids = dest * capacity + ranked
    hit = slot_ids[None, :] == jnp.arange(slots, dtype=jnp.int32)[:, None]
    source = jnp.sum(jnp.where(hit, jnp.arange(tr_rows, dtype=jnp.int32)[None, :], 0), axis=1)
    packed = jnp.take(rows, source, axis=0, mode="clip")
    arrived = lax.all_to_all(packed.reshape(states, capacity, width), "markov", 0, 0, tiled=True)
    node_cols = node_small[5, :nblk * kblk].astype(jnp.int32).reshape(nblk, kblk)
    solved = solve_block(arrived.reshape(slots, width), *node_small[:5], node_blocks, node_cols)
    back = lax.all_to_all(solved.reshape(states, capacity, -1), "markov", 0, 0, tiled=True)
    mine = jnp.take(back.reshape(slots, -1), slot_ids, axis=0, mode="clip")
    return (mine[:, :width].reshape(1, 1, tr_rows, width),
            mine[:, width].reshape(1, 1, tr_rows))


def solution(mesh):
    return jax.shard_map(
        on_device,
        mesh=mesh,
        in_specs=(
            P("week", "markov", None, None),
            P("week", "markov", None, None),
            P("week", "markov", None),
            P("week", "markov", None),
            P("week", "markov", None),
            P("week", "markov", None),
            P("week", "markov", None),
            P("week", "markov", None, None, None, None),
            P("week", "markov", None, None),
        ),
        out_specs=(P("week", "markov", None, None), P("week", "markov", None)),
        check_vma=False,
    )
```

```python
import functools

import jax
import jax.numpy as jnp
from jax import lax
from jax.experimental import pallas as pl
from jax.experimental.pallas import tpu as pltpu
from jax.sharding import PartitionSpec as P

ITERS = 4
BS = 128

dual_step = 0.5
primal_step = 0.5


def shifted(value, axis, steps):
    count = lax.axis_size(axis)
    pairs = [(source, (source + steps) % count) for source in range(count)]
    return lax.ppermute(value, axis, pairs)


def dotb(a, b):
    return lax.dot_general(a, b, (((1,), (0,)), ((), ())), preferred_element_type=jnp.float32)


def split(x):
    hi = x.astype(jnp.bfloat16)
    return hi, (x - hi.astype(jnp.float32)).astype(jnp.bfloat16)


def mm(x, wh, wl):
    xh, xl = split(x)
    return dotb(xh, wh) + dotb(xl, wh) + dotb(xh, wl)


def solve_kernel(nblk, kblk, cols_ref, rows_ref, xi_ref, c_ref, q_ref, g_ref, h_ref, bv_ref,
                 out_ref, base_s, p_s, u_s, v_s, acc_s, fh, fl, ah, al):
    width = nblk * BS
    rows_n = rows_ref.shape[0]

    def lanes(n):
        return slice(n * BS, (n + 1) * BS)

    def col(n, k):
        return cols_ref[n * kblk + k]

    for n in range(nblk):
        hi, lo = split(jnp.concatenate([bv_ref[n, k].T for k in range(kblk)], axis=0))
        fh[n] = hi
        fl[n] = lo
        hi, lo = split(jnp.concatenate([bv_ref[n, k] for k in range(kblk)], axis=1))
        ah[n] = hi
        al[n] = lo

    def mixed_fwd(field_s, n):
        x = jnp.concatenate([field_s[col(n, k)] for k in range(kblk)], axis=1)
        return mm(x, fh[n], fl[n])

    for n in range(nblk):
        s = lanes(n)
        base_s[n] = rows_ref[:, s] + xi_ref[:, s] - g_ref[:, s]
        u_s[n] = jnp.zeros(u_s.shape[1:], jnp.float32)

    for sweep in range(ITERS):
        for n in range(nblk):
            s = lanes(n)
            q = q_ref[:, s]
            shrink = q / (q + dual_step)
            if sweep == 0:
                p_s[n] = (dual_step * base_s[n]) * shrink
            else:
                av = v_s[n] + mixed_fwd(v_s, n)
                p_s[n] = (p_s[n] + dual_step * (base_s[n] - av)) * shrink
        for n in range(nblk):
            acc_s[n] = jnp.zeros(acc_s.shape[1:], jnp.float32)
        for n in range(nblk):
            r = mm(p_s[n], ah[n], al[n])
            for k in range(kblk):
                c = col(n, k)
                acc_s[c] = acc_s[c] + r[:, k * BS:(k + 1) * BS]
        for n in range(nblk):
            s = lanes(n)
            u_old = u_s[n]
            fresh = jnp.clip(u_old + primal_step * (p_s[n] + acc_s[n] - c_ref[:, s]), 0.0, h_ref[:, s])
            v_s[n] = 2.0 * fresh - u_old
            u_s[n] = fresh

    value = jnp.zeros((rows_n, 1), jnp.float32)
    cross = jnp.zeros((rows_n, 1), jnp.float32)
    for n in range(nblk):
        s = lanes(n)
        rows = rows_ref[:, s]
        un = u_s[n]
        gap = rows + xi_ref[:, s] - (un + mixed_fwd(u_s, n)) - g_ref[:, s]
        term = c_ref[:, s] * un + 0.5 * q_ref[:, s] * gap * gap
        value = value + jnp.sum(term, axis=1, keepdims=True)
        pn = p_s[n]
        cross = cross + jnp.sum(pn * rows, axis=1, keepdims=True)
        out_ref[:, s] = pn
    icpt = (value - cross) / width
    out_ref[:, width:] = jnp.broadcast_to(icpt, (rows_n, BS))


def solve_block(rows, inflow, unit_cost, curvature, target, release_cap, block_values, block_cols):
    count, width = rows.shape
    nblk, kblk = block_values.shape[0], block_values.shape[1]
    vec = lambda a: a.reshape(1, width)
    vspec = pl.BlockSpec(memory_space=pltpu.VMEM)
    field = pltpu.VMEM((nblk, count, BS), jnp.float32)
    scratch = [field] * 5
    scratch += [pltpu.VMEM((nblk, kblk * BS, BS), jnp.bfloat16)] * 2
    scratch += [pltpu.VMEM((nblk, BS, kblk * BS), jnp.bfloat16)] * 2
    flops = 2 * count * nblk * kblk * BS * BS * (2 * ITERS) * 3
    return pl.pallas_call(
        functools.partial(solve_kernel, nblk, kblk),
        out_shape=jax.ShapeDtypeStruct((count, width + BS), jnp.float32),
        in_specs=[pl.BlockSpec(memory_space=pltpu.SMEM)] + [vspec] * 7,
        out_specs=vspec,
        scratch_shapes=scratch,
        compiler_params=pltpu.CompilerParams(vmem_limit_bytes=48 * 1024 * 1024),
        cost_estimate=pl.CostEstimate(flops=flops, transcendentals=0,
                                      bytes_accessed=4 * (block_values.size + 3 * rows.size)),
        name="sddp_solve",
    )(block_cols.reshape(-1), rows, vec(inflow), vec(unit_cost), vec(curvature), vec(target),
      vec(release_cap), block_values)


def on_device(trial_states, successor, inflow, unit_cost, curvature, target, release_cap,
              block_values, block_cols):
    states = lax.axis_size("markov")
    tr_rows = trial_states.shape[2]
    width = trial_states.shape[3]
    capacity = 2 * tr_rows // states
    slots = states * capacity
    own_rows = trial_states.reshape(tr_rows, width)
    own_dest = successor.reshape(tr_rows)
    tag = jnp.broadcast_to(own_dest.astype(jnp.float32)[:, None], (tr_rows, BS))
    sent = shifted(jnp.concatenate([own_rows, tag], axis=1), "week", 1)
    rows, dest = sent[:, :width], sent[:, width].astype(jnp.int32)
    marked = (dest[:, None] == jnp.arange(states, dtype=jnp.int32)[None, :]).astype(jnp.int32)
    ranked = jnp.sum(jnp.cumsum(marked, axis=0) * marked, axis=1) - 1
    slot_ids = dest * capacity + ranked
    hit = slot_ids[None, :] == jnp.arange(slots, dtype=jnp.int32)[:, None]
    source = jnp.sum(jnp.where(hit, jnp.arange(tr_rows, dtype=jnp.int32)[None, :], 0), axis=1)
    packed = jnp.take(rows, source, axis=0, mode="clip")
    arrived = lax.all_to_all(packed.reshape(states, capacity, width), "markov", 0, 0, tiled=True)
    solved = solve_block(arrived.reshape(slots, width), inflow.reshape(width),
                         unit_cost.reshape(width), curvature.reshape(width), target.reshape(width),
                         release_cap.reshape(width), block_values[0, 0], block_cols[0, 0])
    back = lax.all_to_all(solved.reshape(states, capacity, -1), "markov", 0, 0, tiled=True)
    mine = jnp.take(back.reshape(slots, -1), slot_ids, axis=0, mode="clip")
    mine = shifted(mine, "week", -1)
    return (mine[:, :width].reshape(1, 1, tr_rows, width),
            mine[:, width].reshape(1, 1, tr_rows))


def solution(mesh):
    return jax.shard_map(
        on_device,
        mesh=mesh,
        in_specs=(
            P("week", "markov", None, None),
            P("week", "markov", None, None),
            P("week", "markov", None),
            P("week", "markov", None),
            P("week", "markov", None),
            P("week", "markov", None),
            P("week", "markov", None),
            P("week", "markov", None, None, None, None),
            P("week", "markov", None, None),
        ),
        out_specs=(P("week", "markov", None, None), P("week", "markov", None)),
        check_vma=False,
    )
```

```python
import functools

import jax
import jax.numpy as jnp
from jax import lax
from jax.experimental import pallas as pl
from jax.experimental.pallas import tpu as pltpu
from jax.sharding import PartitionSpec as P

ITERS = 4
BS = 128

dual_step = 0.5
primal_step = 0.5


def shifted(value, axis, steps):
    count = lax.axis_size(axis)
    pairs = [(source, (source + steps) % count) for source in range(count)]
    return lax.ppermute(value, axis, pairs)


def dotb(a, b):
    return lax.dot_general(a, b, (((1,), (0,)), ((), ())), preferred_element_type=jnp.float32)


def split(x):
    hi = x.astype(jnp.bfloat16)
    return hi, (x - hi.astype(jnp.float32)).astype(jnp.bfloat16)


def mm(x, wh, wl):
    xh, xl = split(x)
    return dotb(xh, wh) + dotb(xl, wh) + dotb(xh, wl)


def solve_kernel(nblk, kblk, cols_ref, rows_ref, xi_ref, c_ref, q_ref, g_ref, h_ref, bv_ref,
                 out_ref, base_s, p_s, u_s, v_s, acc_s, fh, fl, ah, al):
    width = nblk * BS
    rows_n = rows_ref.shape[0]

    def lanes(n):
        return slice(n * BS, (n + 1) * BS)

    def col(n, k):
        return cols_ref[n * kblk + k]

    for n in range(nblk):
        hi, lo = split(jnp.concatenate([bv_ref[n, k].T for k in range(kblk)], axis=0))
        fh[n] = hi
        fl[n] = lo
        hi, lo = split(jnp.concatenate([bv_ref[n, k] for k in range(kblk)], axis=1))
        ah[n] = hi
        al[n] = lo

    def mixed_fwd(field_s, n):
        x = jnp.concatenate([field_s[col(n, k)] for k in range(kblk)], axis=1)
        return mm(x, fh[n], fl[n])

    for n in range(nblk):
        s = lanes(n)
        base_s[n] = rows_ref[:, s] + xi_ref[:, s] - g_ref[:, s]
        u_s[n] = jnp.zeros(u_s.shape[1:], jnp.float32)

    for sweep in range(ITERS):
        for n in range(nblk):
            s = lanes(n)
            q = q_ref[:, s]
            shrink = q / (q + dual_step)
            if sweep == 0:
                p_s[n] = (dual_step * base_s[n]) * shrink
            else:
                av = v_s[n] + mixed_fwd(v_s, n)
                p_s[n] = (p_s[n] + dual_step * (base_s[n] - av)) * shrink
        for n in range(nblk):
            acc_s[n] = jnp.zeros(acc_s.shape[1:], jnp.float32)
        for n in range(nblk):
            r = mm(p_s[n], ah[n], al[n])
            for k in range(kblk):
                c = col(n, k)
                acc_s[c] = acc_s[c] + r[:, k * BS:(k + 1) * BS]
        for n in range(nblk):
            s = lanes(n)
            u_old = u_s[n]
            fresh = jnp.clip(u_old + primal_step * (p_s[n] + acc_s[n] - c_ref[:, s]), 0.0, h_ref[:, s])
            v_s[n] = 2.0 * fresh - u_old
            u_s[n] = fresh

    value = jnp.zeros((rows_n, 1), jnp.float32)
    cross = jnp.zeros((rows_n, 1), jnp.float32)
    for n in range(nblk):
        s = lanes(n)
        rows = rows_ref[:, s]
        un = u_s[n]
        gap = rows + xi_ref[:, s] - (un + mixed_fwd(u_s, n)) - g_ref[:, s]
        term = c_ref[:, s] * un + 0.5 * q_ref[:, s] * gap * gap
        value = value + jnp.sum(term, axis=1, keepdims=True)
        pn = p_s[n]
        cross = cross + jnp.sum(pn * rows, axis=1, keepdims=True)
        out_ref[:, :, s] = pn.reshape(out_ref.shape[0], out_ref.shape[1], BS)
    icpt = (value - cross) / width
    out_ref[:, :, width:] = jnp.broadcast_to(icpt, (rows_n, BS)).reshape(out_ref.shape[0], out_ref.shape[1], BS)


def solve_block(rows, inflow, unit_cost, curvature, target, release_cap, block_values, block_cols,
                groups):
    count, width = rows.shape
    nblk, kblk = block_values.shape[0], block_values.shape[1]
    vec = lambda a: a.reshape(1, width)
    vspec = pl.BlockSpec(memory_space=pltpu.VMEM)
    field = pltpu.VMEM((nblk, count, BS), jnp.float32)
    scratch = [field] * 5
    scratch += [pltpu.VMEM((nblk, kblk * BS, BS), jnp.bfloat16)] * 2
    scratch += [pltpu.VMEM((nblk, BS, kblk * BS), jnp.bfloat16)] * 2
    flops = 2 * count * nblk * kblk * BS * BS * (2 * ITERS) * 3
    return pl.pallas_call(
        functools.partial(solve_kernel, nblk, kblk),
        out_shape=jax.ShapeDtypeStruct((groups, count // groups, width + BS), jnp.float32),
        in_specs=[pl.BlockSpec(memory_space=pltpu.SMEM)] + [vspec] * 7,
        out_specs=vspec,
        scratch_shapes=scratch,
        compiler_params=pltpu.CompilerParams(vmem_limit_bytes=48 * 1024 * 1024),
        cost_estimate=pl.CostEstimate(flops=flops, transcendentals=0,
                                      bytes_accessed=4 * (block_values.size + 3 * rows.size)),
        name="sddp_solve",
    )(block_cols.reshape(-1), rows, vec(inflow), vec(unit_cost), vec(curvature), vec(target),
      vec(release_cap), block_values)


def on_device(trial_states, successor, inflow, unit_cost, curvature, target, release_cap,
              block_values, block_cols):
    states = lax.axis_size("markov")
    tr_rows = trial_states.shape[2]
    width = trial_states.shape[3]
    capacity = 2 * tr_rows // states
    slots = states * capacity
    own_rows = trial_states.reshape(tr_rows, width)
    own_dest = successor.reshape(tr_rows)
    tag = jnp.broadcast_to(own_dest.astype(jnp.float32)[:, None], (tr_rows, BS))
    sent = shifted(jnp.concatenate([own_rows, tag], axis=1), "week", 1)
    rows, dest = sent[:, :width], sent[:, width].astype(jnp.int32)
    marked = (dest[:, None] == jnp.arange(states, dtype=jnp.int32)[None, :]).astype(jnp.int32)
    ranked = jnp.sum(jnp.cumsum(marked, axis=0) * marked, axis=1) - 1
    slot_ids = dest * capacity + ranked
    hit = slot_ids[None, :] == jnp.arange(slots, dtype=jnp.int32)[:, None]
    source = jnp.sum(jnp.where(hit, jnp.arange(tr_rows, dtype=jnp.int32)[None, :], 0), axis=1)
    packed = jnp.take(rows, source.reshape(states, capacity), axis=0, mode="clip")
    arrived = lax.all_to_all(packed, "markov", 0, 0, tiled=True)
    solved = solve_block(arrived.reshape(slots, width), inflow.reshape(width),
                         unit_cost.reshape(width), curvature.reshape(width), target.reshape(width),
                         release_cap.reshape(width), block_values[0, 0], block_cols[0, 0], states)
    back = lax.all_to_all(solved, "markov", 0, 0, tiled=True)
    mine = back.at[dest, ranked].get(mode="clip")
    mine = shifted(mine, "week", -1)
    return (mine[:, :width].reshape(1, 1, tr_rows, width),
            mine[:, width].reshape(1, 1, tr_rows))


def solution(mesh):
    return jax.shard_map(
        on_device,
        mesh=mesh,
        in_specs=(
            P("week", "markov", None, None),
            P("week", "markov", None, None),
            P("week", "markov", None),
            P("week", "markov", None),
            P("week", "markov", None),
            P("week", "markov", None),
            P("week", "markov", None),
            P("week", "markov", None, None, None, None),
            P("week", "markov", None, None),
        ),
        out_specs=(P("week", "markov", None, None), P("week", "markov", None)),
        check_vma=False,
    )
```

```python
import functools

import jax
import jax.numpy as jnp
from jax import lax
from jax.experimental import pallas as pl
from jax.experimental.pallas import tpu as pltpu
from jax.sharding import PartitionSpec as P

ITERS = 4
BS = 128

dual_step = 0.5
primal_step = 0.5


def shifted(value, axis, steps):
    count = lax.axis_size(axis)
    pairs = [(source, (source + steps) % count) for source in range(count)]
    return lax.ppermute(value, axis, pairs)


def dotb(a, b):
    return lax.dot_general(a, b, (((1,), (0,)), ((), ())), preferred_element_type=jnp.float32)


def split(x):
    hi = x.astype(jnp.bfloat16)
    return hi, (x - hi.astype(jnp.float32)).astype(jnp.bfloat16)


def mm(x, wh, wl):
    xh, xl = split(x)
    return dotb(xh, wh) + dotb(xl, wh) + dotb(xh, wl)


def solve_kernel(nblk, kblk, cols_ref, rows_ref, xi_ref, c_ref, q_ref, g_ref, h_ref, bv_ref,
                 out_ref, base_s, p_s, u_s, v_s, acc_s, fh, fl, ah, al):
    width = nblk * BS
    rows_n = rows_ref.shape[0]

    def lanes(n):
        return slice(n * BS, (n + 1) * BS)

    def col(n, k):
        return cols_ref[n * kblk + k]

    for n in range(nblk):
        hi, lo = split(jnp.concatenate([bv_ref[n, k].T for k in range(kblk)], axis=0))
        fh[n] = hi
        fl[n] = lo
        hi, lo = split(jnp.concatenate([bv_ref[n, k] for k in range(kblk)], axis=1))
        ah[n] = hi
        al[n] = lo

    def mixed_fwd(field_s, n):
        x = jnp.concatenate([field_s[col(n, k)] for k in range(kblk)], axis=1)
        return mm(x, fh[n], fl[n])

    for n in range(nblk):
        s = lanes(n)
        base_s[n] = rows_ref[:, s] + xi_ref[:, s] - g_ref[:, s]
        u_s[n] = jnp.zeros(u_s.shape[1:], jnp.float32)

    for sweep in range(ITERS):
        for n in range(nblk):
            s = lanes(n)
            q = q_ref[:, s]
            shrink = q / (q + dual_step)
            if sweep == 0:
                p_s[n] = (dual_step * base_s[n]) * shrink
            else:
                av = v_s[n] + mixed_fwd(v_s, n)
                p_s[n] = (p_s[n] + dual_step * (base_s[n] - av)) * shrink
        for n in range(nblk):
            acc_s[n] = jnp.zeros(acc_s.shape[1:], jnp.float32)
        for n in range(nblk):
            r = mm(p_s[n], ah[n], al[n])
            for k in range(kblk):
                c = col(n, k)
                acc_s[c] = acc_s[c] + r[:, k * BS:(k + 1) * BS]
        for n in range(nblk):
            s = lanes(n)
            u_old = u_s[n]
            fresh = jnp.clip(u_old + primal_step * (p_s[n] + acc_s[n] - c_ref[:, s]), 0.0, h_ref[:, s])
            v_s[n] = 2.0 * fresh - u_old
            u_s[n] = fresh

    value = jnp.zeros((rows_n, 1), jnp.float32)
    cross = jnp.zeros((rows_n, 1), jnp.float32)
    for n in range(nblk):
        s = lanes(n)
        rows = rows_ref[:, s]
        un = u_s[n]
        gap = rows + xi_ref[:, s] - (un + mixed_fwd(u_s, n)) - g_ref[:, s]
        term = c_ref[:, s] * un + 0.5 * q_ref[:, s] * gap * gap
        value = value + jnp.sum(term, axis=1, keepdims=True)
        pn = p_s[n]
        cross = cross + jnp.sum(pn * rows, axis=1, keepdims=True)
        out_ref[:, :, s] = pn.reshape(out_ref.shape[0], out_ref.shape[1], BS)
    icpt = (value - cross) / width
    out_ref[:, :, width:] = jnp.broadcast_to(icpt, (rows_n, BS)).reshape(out_ref.shape[0], out_ref.shape[1], BS)


def solve_block(rows, inflow, unit_cost, curvature, target, release_cap, block_values, block_cols,
                groups):
    count, width = rows.shape
    nblk, kblk = block_values.shape[0], block_values.shape[1]
    vec = lambda a: a.reshape(1, width)
    vspec = pl.BlockSpec(memory_space=pltpu.VMEM)
    field = pltpu.VMEM((nblk, count, BS), jnp.float32)
    scratch = [field] * 5
    scratch += [pltpu.VMEM((nblk, kblk * BS, BS), jnp.bfloat16)] * 2
    scratch += [pltpu.VMEM((nblk, BS, kblk * BS), jnp.bfloat16)] * 2
    flops = 2 * count * nblk * kblk * BS * BS * (2 * ITERS) * 3
    return pl.pallas_call(
        functools.partial(solve_kernel, nblk, kblk),
        out_shape=jax.ShapeDtypeStruct((groups, count // groups, width + BS), jnp.float32),
        in_specs=[pl.BlockSpec(memory_space=pltpu.SMEM)] + [vspec] * 7,
        out_specs=vspec,
        scratch_shapes=scratch,
        compiler_params=pltpu.CompilerParams(vmem_limit_bytes=48 * 1024 * 1024),
        cost_estimate=pl.CostEstimate(flops=flops, transcendentals=0,
                                      bytes_accessed=4 * (block_values.size + 3 * rows.size)),
        name="sddp_solve",
    )(block_cols.reshape(-1), rows, vec(inflow), vec(unit_cost), vec(curvature), vec(target),
      vec(release_cap), block_values)


def on_device(trial_states, successor, inflow, unit_cost, curvature, target, release_cap,
              block_values, block_cols):
    states = lax.axis_size("markov")
    tr_rows = trial_states.shape[2]
    width = trial_states.shape[3]
    capacity = 2 * tr_rows // states
    slots = states * capacity
    own_rows = trial_states.reshape(tr_rows, width)
    own_dest = successor.reshape(tr_rows)
    rows, dest = shifted((own_rows, own_dest), "week", 1)
    marked = (dest[:, None] == jnp.arange(states, dtype=jnp.int32)[None, :]).astype(jnp.int32)
    ranked = jnp.sum(jnp.cumsum(marked, axis=0) * marked, axis=1) - 1
    slot_ids = dest * capacity + ranked
    hit = slot_ids[None, :] == jnp.arange(slots, dtype=jnp.int32)[:, None]
    source = jnp.sum(jnp.where(hit, jnp.arange(tr_rows, dtype=jnp.int32)[None, :], 0), axis=1)
    packed = jnp.take(rows, source.reshape(states, capacity), axis=0, mode="clip")
    arrived = lax.all_to_all(packed, "markov", 0, 0, tiled=True)
    solved = solve_block(arrived.reshape(slots, width), inflow.reshape(width),
                         unit_cost.reshape(width), curvature.reshape(width), target.reshape(width),
                         release_cap.reshape(width), block_values[0, 0], block_cols[0, 0], states)
    back = lax.all_to_all(solved, "markov", 0, 0, tiled=True)
    mine = back.at[dest, ranked].get(mode="clip")
    mine = shifted(mine, "week", -1)
    return (mine[:, :width].reshape(1, 1, tr_rows, width),
            mine[:, width].reshape(1, 1, tr_rows))


def solution(mesh):
    return jax.shard_map(
        on_device,
        mesh=mesh,
        in_specs=(
            P("week", "markov", None, None),
            P("week", "markov", None, None),
            P("week", "markov", None),
            P("week", "markov", None),
            P("week", "markov", None),
            P("week", "markov", None),
            P("week", "markov", None),
            P("week", "markov", None, None, None, None),
            P("week", "markov", None, None),
        ),
        out_specs=(P("week", "markov", None, None), P("week", "markov", None)),
        check_vma=False,
    )
```

```python
import functools

import jax
import jax.numpy as jnp
from jax import lax
from jax.experimental import pallas as pl
from jax.experimental.pallas import tpu as pltpu
from jax.sharding import PartitionSpec as P

ITERS = 4
BS = 128

dual_step = 0.5
primal_step = 0.5


def shifted(value, axis, steps):
    count = lax.axis_size(axis)
    pairs = [(source, (source + steps) % count) for source in range(count)]
    return lax.ppermute(value, axis, pairs)


def dotb(a, b):
    return lax.dot_general(a, b, (((1,), (0,)), ((), ())), preferred_element_type=jnp.float32)


def split(x):
    hi = x.astype(jnp.bfloat16)
    return hi, (x - hi.astype(jnp.float32)).astype(jnp.bfloat16)


def mm(x, wh, wl):
    xh, xl = split(x)
    return dotb(xh, wh) + dotb(xl, wh) + dotb(xh, wl)


def solve_kernel(nblk, kblk, cols_ref, rows_ref, xi_ref, c_ref, q_ref, g_ref, h_ref, bv_ref,
                 out_ref, base_s, p_s, u_s, v_s, acc_s, fh, fl, ah, al):
    width = nblk * BS
    rows_n = rows_ref.shape[0]

    def lanes(n):
        return slice(n * BS, (n + 1) * BS)

    def col(n, k):
        return cols_ref[n * kblk + k]

    for n in range(nblk):
        hi, lo = split(jnp.concatenate([bv_ref[n, k].T for k in range(kblk)], axis=0))
        fh[n] = hi
        fl[n] = lo
        hi, lo = split(jnp.concatenate([bv_ref[n, k] for k in range(kblk)], axis=1))
        ah[n] = hi
        al[n] = lo

    def mixed_fwd(field_s, n):
        x = jnp.concatenate([field_s[col(n, k)] for k in range(kblk)], axis=1)
        return mm(x, fh[n], fl[n])

    for n in range(nblk):
        s = lanes(n)
        base_s[n] = rows_ref[:, s] + xi_ref[:, s] - g_ref[:, s]
        u_s[n] = jnp.zeros(u_s.shape[1:], jnp.float32)

    for sweep in range(ITERS):
        for n in range(nblk):
            s = lanes(n)
            q = q_ref[:, s]
            shrink = q / (q + dual_step)
            if sweep == 0:
                p_s[n] = (dual_step * base_s[n]) * shrink
            else:
                av = v_s[n] + mixed_fwd(v_s, n)
                p_s[n] = (p_s[n] + dual_step * (base_s[n] - av)) * shrink
        for n in range(nblk):
            acc_s[n] = jnp.zeros(acc_s.shape[1:], jnp.float32)
        for n in range(nblk):
            r = mm(p_s[n], ah[n], al[n])
            for k in range(kblk):
                c = col(n, k)
                acc_s[c] = acc_s[c] + r[:, k * BS:(k + 1) * BS]
        for n in range(nblk):
            s = lanes(n)
            u_old = u_s[n]
            fresh = jnp.clip(u_old + primal_step * (p_s[n] + acc_s[n] - c_ref[:, s]), 0.0, h_ref[:, s])
            v_s[n] = 2.0 * fresh - u_old
            u_s[n] = fresh

    value = jnp.zeros((rows_n, 1), jnp.float32)
    cross = jnp.zeros((rows_n, 1), jnp.float32)
    for n in range(nblk):
        s = lanes(n)
        rows = rows_ref[:, s]
        un = u_s[n]
        gap = rows + xi_ref[:, s] - (un + mixed_fwd(u_s, n)) - g_ref[:, s]
        term = c_ref[:, s] * un + 0.5 * q_ref[:, s] * gap * gap
        value = value + jnp.sum(term, axis=1, keepdims=True)
        pn = p_s[n]
        cross = cross + jnp.sum(pn * rows, axis=1, keepdims=True)
        out_ref[:, :, s] = pn.reshape(out_ref.shape[0], out_ref.shape[1], BS)
    icpt = (value - cross) / width
    out_ref[:, :, width:] = jnp.broadcast_to(icpt, (rows_n, BS)).reshape(out_ref.shape[0], out_ref.shape[1], BS)


def solve_block(rows, inflow, unit_cost, curvature, target, release_cap, block_values, block_cols,
                groups):
    count, width = rows.shape
    nblk, kblk = block_values.shape[0], block_values.shape[1]
    vec = lambda a: a.reshape(1, width)
    vspec = pl.BlockSpec(memory_space=pltpu.VMEM)
    field = pltpu.VMEM((nblk, count, BS), jnp.float32)
    scratch = [field] * 5
    scratch += [pltpu.VMEM((nblk, kblk * BS, BS), jnp.bfloat16)] * 2
    scratch += [pltpu.VMEM((nblk, BS, kblk * BS), jnp.bfloat16)] * 2
    flops = 2 * count * nblk * kblk * BS * BS * (2 * ITERS) * 3
    return pl.pallas_call(
        functools.partial(solve_kernel, nblk, kblk),
        out_shape=jax.ShapeDtypeStruct((groups, count // groups, width + BS), jnp.float32),
        in_specs=[pl.BlockSpec(memory_space=pltpu.SMEM)] + [vspec] * 7,
        out_specs=vspec,
        scratch_shapes=scratch,
        compiler_params=pltpu.CompilerParams(vmem_limit_bytes=48 * 1024 * 1024),
        cost_estimate=pl.CostEstimate(flops=flops, transcendentals=0,
                                      bytes_accessed=4 * (block_values.size + 3 * rows.size)),
        name="sddp_solve",
    )(block_cols.reshape(-1), rows, vec(inflow), vec(unit_cost), vec(curvature), vec(target),
      vec(release_cap), block_values)


def pack_kernel(states, capacity, source_ref, rows_ref, out_ref):
    for i in range(states):
        for j in range(capacity):
            src = source_ref[i * capacity + j]
            out_ref[i, pl.ds(j, 1), :] = rows_ref[pl.ds(src, 1), :]


def pack_slots(rows, source, states, capacity):
    width = rows.shape[1]
    return pl.pallas_call(
        functools.partial(pack_kernel, states, capacity),
        out_shape=jax.ShapeDtypeStruct((states, capacity, width), jnp.float32),
        in_specs=[pl.BlockSpec(memory_space=pltpu.SMEM), pl.BlockSpec(memory_space=pltpu.VMEM)],
        out_specs=pl.BlockSpec(memory_space=pltpu.VMEM),
        cost_estimate=pl.CostEstimate(flops=0, transcendentals=0, bytes_accessed=12 * rows.size),
        name="sddp_pack",
    )(source, rows)


def on_device(trial_states, successor, inflow, unit_cost, curvature, target, release_cap,
              block_values, block_cols):
    states = lax.axis_size("markov")
    tr_rows = trial_states.shape[2]
    width = trial_states.shape[3]
    capacity = 2 * tr_rows // states
    slots = states * capacity
    own_rows = trial_states.reshape(tr_rows, width)
    own_dest = successor.reshape(tr_rows)
    tag = jnp.broadcast_to(own_dest.astype(jnp.float32)[:, None], (tr_rows, BS))
    sent = shifted(jnp.concatenate([own_rows, tag], axis=1), "week", 1)
    rows, dest = sent[:, :width], sent[:, width].astype(jnp.int32)
    marked = (dest[:, None] == jnp.arange(states, dtype=jnp.int32)[None, :]).astype(jnp.int32)
    ranked = jnp.sum(jnp.cumsum(marked, axis=0) * marked, axis=1) - 1
    slot_ids = dest * capacity + ranked
    hit = slot_ids[None, :] == jnp.arange(slots, dtype=jnp.int32)[:, None]
    source = jnp.sum(jnp.where(hit, jnp.arange(tr_rows, dtype=jnp.int32)[None, :], 0), axis=1)
    packed = pack_slots(rows, source, states, capacity)
    arrived = lax.all_to_all(packed, "markov", 0, 0, tiled=True)
    solved = solve_block(arrived.reshape(slots, width), inflow.reshape(width),
                         unit_cost.reshape(width), curvature.reshape(width), target.reshape(width),
                         release_cap.reshape(width), block_values[0, 0], block_cols[0, 0], states)
    back = lax.all_to_all(solved, "markov", 0, 0, tiled=True)
    mine = back.at[dest, ranked].get(mode="clip")
    mine = shifted(mine, "week", -1)
    return (mine[:, :width].reshape(1, 1, tr_rows, width),
            mine[:, width].reshape(1, 1, tr_rows))


def solution(mesh):
    return jax.shard_map(
        on_device,
        mesh=mesh,
        in_specs=(
            P("week", "markov", None, None),
            P("week", "markov", None, None),
            P("week", "markov", None),
            P("week", "markov", None),
            P("week", "markov", None),
            P("week", "markov", None),
            P("week", "markov", None),
            P("week", "markov", None, None, None, None),
            P("week", "markov", None, None),
        ),
        out_specs=(P("week", "markov", None, None), P("week", "markov", None)),
        check_vma=False,
    )
```

```python
import functools

import jax
import jax.numpy as jnp
from jax import lax
from jax.experimental import pallas as pl
from jax.experimental.pallas import tpu as pltpu
from jax.sharding import PartitionSpec as P

ITERS = 4
BS = 128

dual_step = 0.5
primal_step = 0.5


def shifted(value, axis, steps):
    count = lax.axis_size(axis)
    pairs = [(source, (source + steps) % count) for source in range(count)]
    return lax.ppermute(value, axis, pairs)


def dotb(a, b):
    return lax.dot_general(a, b, (((1,), (0,)), ((), ())), preferred_element_type=jnp.float32)


def split(x):
    hi = x.astype(jnp.bfloat16)
    return hi, (x - hi.astype(jnp.float32)).astype(jnp.bfloat16)


def mm(x, wh, wl):
    xh, xl = split(x)
    return dotb(xh, wh) + dotb(xl, wh) + dotb(xh, wl)


def solve_kernel(nblk, kblk, cols_ref, rows_ref, xi_ref, c_ref, q_ref, g_ref, h_ref, bv_ref,
                 out_ref, base_s, p_s, u_s, v_s, acc_s, spread_s, fh, fl, ah, al):
    width = nblk * BS
    rows_n = rows_ref.shape[0]

    def lanes(n):
        return slice(n * BS, (n + 1) * BS)

    def col(n, k):
        return cols_ref[n * kblk + k]

    for n in range(nblk):
        hi, lo = split(jnp.concatenate([bv_ref[n, k].T for k in range(kblk)], axis=0))
        fh[n] = hi
        fl[n] = lo
        hi, lo = split(jnp.concatenate([bv_ref[n, k] for k in range(kblk)], axis=1))
        ah[n] = hi
        al[n] = lo

    def mixed_fwd(field_s, n):
        x = jnp.concatenate([field_s[col(n, k)] for k in range(kblk)], axis=1)
        return mm(x, fh[n], fl[n])

    for n in range(nblk):
        s = lanes(n)
        base_s[n] = rows_ref[:, s] + xi_ref[:, s] - g_ref[:, s]
        u_s[n] = jnp.zeros(u_s.shape[1:], jnp.float32)

    for sweep in range(ITERS):
        for n in range(nblk):
            s = lanes(n)
            q = q_ref[:, s]
            shrink = q / (q + dual_step)
            if sweep == 0:
                p_s[n] = (dual_step * base_s[n]) * shrink
            else:
                av = v_s[n] + mixed_fwd(v_s, n)
                p_s[n] = (p_s[n] + dual_step * (base_s[n] - av)) * shrink
        for n in range(nblk):
            spread_s[n] = mm(p_s[n], ah[n], al[n])
        for n in range(nblk):
            acc_s[n] = p_s[n]
        for n in range(nblk):
            for k in range(kblk):
                c = col(n, k)
                acc_s[c] = acc_s[c] + spread_s[n, :, k * BS:(k + 1) * BS]
        for n in range(nblk):
            s = lanes(n)
            u_old = u_s[n]
            fresh = jnp.clip(u_old + primal_step * (acc_s[n] - c_ref[:, s]), 0.0, h_ref[:, s])
            v_s[n] = 2.0 * fresh - u_old
            u_s[n] = fresh

    value = jnp.zeros((rows_n, BS), jnp.float32)
    cross = jnp.zeros((rows_n, BS), jnp.float32)
    for n in range(nblk):
        s = lanes(n)
        rows = rows_ref[:, s]
        un = u_s[n]
        gap = rows + xi_ref[:, s] - (un + mixed_fwd(u_s, n)) - g_ref[:, s]
        value = value + (c_ref[:, s] * un + 0.5 * q_ref[:, s] * gap * gap)
        pn = p_s[n]
        cross = cross + pn * rows
        out_ref[:, :, s] = pn.reshape(out_ref.shape[0], out_ref.shape[1], BS)
    icpt = (jnp.sum(value, axis=1, keepdims=True) - jnp.sum(cross, axis=1, keepdims=True)) / width
    out_ref[:, :, width:] = jnp.broadcast_to(icpt, (rows_n, BS)).reshape(out_ref.shape[0], out_ref.shape[1], BS)


def solve_block(rows, inflow, unit_cost, curvature, target, release_cap, block_values, block_cols,
                groups):
    count, width = rows.shape
    nblk, kblk = block_values.shape[0], block_values.shape[1]
    vec = lambda a: a.reshape(1, width)
    vspec = pl.BlockSpec(memory_space=pltpu.VMEM)
    field = pltpu.VMEM((nblk, count, BS), jnp.float32)
    scratch = [field] * 5 + [pltpu.VMEM((nblk, count, kblk * BS), jnp.float32)]
    scratch += [pltpu.VMEM((nblk, kblk * BS, BS), jnp.bfloat16)] * 2
    scratch += [pltpu.VMEM((nblk, BS, kblk * BS), jnp.bfloat16)] * 2
    flops = 2 * count * nblk * kblk * BS * BS * (2 * ITERS) * 3
    return pl.pallas_call(
        functools.partial(solve_kernel, nblk, kblk),
        out_shape=jax.ShapeDtypeStruct((groups, count // groups, width + BS), jnp.float32),
        in_specs=[pl.BlockSpec(memory_space=pltpu.SMEM)] + [vspec] * 7,
        out_specs=vspec,
        scratch_shapes=scratch,
        compiler_params=pltpu.CompilerParams(vmem_limit_bytes=48 * 1024 * 1024),
        cost_estimate=pl.CostEstimate(flops=flops, transcendentals=0,
                                      bytes_accessed=4 * (block_values.size + 3 * rows.size)),
        name="sddp_solve",
    )(block_cols.reshape(-1), rows, vec(inflow), vec(unit_cost), vec(curvature), vec(target),
      vec(release_cap), block_values)


def on_device(trial_states, successor, inflow, unit_cost, curvature, target, release_cap,
              block_values, block_cols):
    states = lax.axis_size("markov")
    tr_rows = trial_states.shape[2]
    width = trial_states.shape[3]
    capacity = 2 * tr_rows // states
    slots = states * capacity
    own_rows = trial_states.reshape(tr_rows, width)
    own_dest = successor.reshape(tr_rows)
    tag = jnp.broadcast_to(own_dest.astype(jnp.float32)[:, None], (tr_rows, BS))
    sent = shifted(jnp.concatenate([own_rows, tag], axis=1), "week", 1)
    rows, dest = sent[:, :width], sent[:, width].astype(jnp.int32)
    marked = (dest[:, None] == jnp.arange(states, dtype=jnp.int32)[None, :]).astype(jnp.int32)
    ranked = jnp.sum(jnp.cumsum(marked, axis=0) * marked, axis=1) - 1
    slot_ids = dest * capacity + ranked
    hit = slot_ids[None, :] == jnp.arange(slots, dtype=jnp.int32)[:, None]
    source = jnp.sum(jnp.where(hit, jnp.arange(tr_rows, dtype=jnp.int32)[None, :], 0), axis=1)
    packed = jnp.take(rows, source.reshape(states, capacity), axis=0, mode="clip")
    arrived = lax.all_to_all(packed, "markov", 0, 0, tiled=True)
    solved = solve_block(arrived.reshape(slots, width), inflow.reshape(width),
                         unit_cost.reshape(width), curvature.reshape(width), target.reshape(width),
                         release_cap.reshape(width), block_values[0, 0], block_cols[0, 0], states)
    back = lax.all_to_all(solved, "markov", 0, 0, tiled=True)
    mine = back.at[dest, ranked].get(mode="clip")
    mine = shifted(mine, "week", -1)
    return (mine[:, :width].reshape(1, 1, tr_rows, width),
            mine[:, width].reshape(1, 1, tr_rows))


def solution(mesh):
    return jax.shard_map(
        on_device,
        mesh=mesh,
        in_specs=(
            P("week", "markov", None, None),
            P("week", "markov", None, None),
            P("week", "markov", None),
            P("week", "markov", None),
            P("week", "markov", None),
            P("week", "markov", None),
            P("week", "markov", None),
            P("week", "markov", None, None, None, None),
            P("week", "markov", None, None),
        ),
        out_specs=(P("week", "markov", None, None), P("week", "markov", None)),
        check_vma=False,
    )
```

```python
import functools

import jax
import jax.numpy as jnp
from jax import lax
from jax.experimental import pallas as pl
from jax.experimental.pallas import tpu as pltpu
from jax.sharding import PartitionSpec as P

ITERS = 4
BS = 128

dual_step = 0.5
primal_step = 0.5


def shifted(value, axis, steps):
    count = lax.axis_size(axis)
    pairs = [(source, (source + steps) % count) for source in range(count)]
    return lax.ppermute(value, axis, pairs)


def dotb(a, b):
    return lax.dot_general(a, b, (((1,), (0,)), ((), ())), preferred_element_type=jnp.float32)


def split(x):
    hi = x.astype(jnp.bfloat16)
    return hi, (x - hi.astype(jnp.float32)).astype(jnp.bfloat16)


def mm(x, w3):
    xh, xl = split(x)
    return dotb(jnp.concatenate([xh, xl, xh], axis=1), w3)


def solve_kernel(nblk, kblk, cols_ref, rows_ref, xi_ref, c_ref, q_ref, g_ref, h_ref, bv_ref,
                 out_ref, base_s, p_s, u_s, v_s, acc_s, spread_s, fw, aw):
    width = nblk * BS
    rows_n = rows_ref.shape[0]

    def lanes(n):
        return slice(n * BS, (n + 1) * BS)

    def col(n, k):
        return cols_ref[n * kblk + k]

    for n in range(nblk):
        hi, lo = split(jnp.concatenate([bv_ref[n, k].T for k in range(kblk)], axis=0))
        fw[n] = jnp.concatenate([hi, hi, lo], axis=0)
        hi, lo = split(jnp.concatenate([bv_ref[n, k] for k in range(kblk)], axis=1))
        aw[n] = jnp.concatenate([hi, hi, lo], axis=0)

    def mixed_fwd(field_s, n):
        x = jnp.concatenate([field_s[col(n, k)] for k in range(kblk)], axis=1)
        return mm(x, fw[n])

    for n in range(nblk):
        s = lanes(n)
        base_s[n] = rows_ref[:, s] + xi_ref[:, s] - g_ref[:, s]
        u_s[n] = jnp.zeros(u_s.shape[1:], jnp.float32)

    for sweep in range(ITERS):
        for n in range(nblk):
            s = lanes(n)
            q = q_ref[:, s]
            shrink = q / (q + dual_step)
            if sweep == 0:
                p_s[n] = (dual_step * base_s[n]) * shrink
            else:
                av = v_s[n] + mixed_fwd(v_s, n)
                p_s[n] = (p_s[n] + dual_step * (base_s[n] - av)) * shrink
        for n in range(nblk):
            spread_s[n] = mm(p_s[n], aw[n])
        for n in range(nblk):
            acc_s[n] = p_s[n]
        for n in range(nblk):
            for k in range(kblk):
                c = col(n, k)
                acc_s[c] = acc_s[c] + spread_s[n, :, k * BS:(k + 1) * BS]
        for n in range(nblk):
            s = lanes(n)
            u_old = u_s[n]
            fresh = jnp.clip(u_old + primal_step * (acc_s[n] - c_ref[:, s]), 0.0, h_ref[:, s])
            v_s[n] = 2.0 * fresh - u_old
            u_s[n] = fresh

    value = jnp.zeros((rows_n, BS), jnp.float32)
    cross = jnp.zeros((rows_n, BS), jnp.float32)
    for n in range(nblk):
        s = lanes(n)
        rows = rows_ref[:, s]
        un = u_s[n]
        gap = rows + xi_ref[:, s] - (un + mixed_fwd(u_s, n)) - g_ref[:, s]
        value = value + (c_ref[:, s] * un + 0.5 * q_ref[:, s] * gap * gap)
        pn = p_s[n]
        cross = cross + pn * rows
        out_ref[:, :, s] = pn.reshape(out_ref.shape[0], out_ref.shape[1], BS)
    icpt = (jnp.sum(value, axis=1, keepdims=True) - jnp.sum(cross, axis=1, keepdims=True)) / width
    out_ref[:, :, width:] = jnp.broadcast_to(icpt, (rows_n, BS)).reshape(out_ref.shape[0], out_ref.shape[1], BS)


def solve_block(rows, inflow, unit_cost, curvature, target, release_cap, block_values, block_cols,
                groups):
    count, width = rows.shape
    nblk, kblk = block_values.shape[0], block_values.shape[1]
    vec = lambda a: a.reshape(1, width)
    vspec = pl.BlockSpec(memory_space=pltpu.VMEM)
    field = pltpu.VMEM((nblk, count, BS), jnp.float32)
    scratch = [field] * 5 + [pltpu.VMEM((nblk, count, kblk * BS), jnp.float32)]
    scratch += [pltpu.VMEM((nblk, 3 * kblk * BS, BS), jnp.bfloat16)]
    scratch += [pltpu.VMEM((nblk, 3 * BS, kblk * BS), jnp.bfloat16)]
    flops = 2 * count * nblk * kblk * BS * BS * (2 * ITERS) * 3
    return pl.pallas_call(
        functools.partial(solve_kernel, nblk, kblk),
        out_shape=jax.ShapeDtypeStruct((groups, count // groups, width + BS), jnp.float32),
        in_specs=[pl.BlockSpec(memory_space=pltpu.SMEM)] + [vspec] * 7,
        out_specs=vspec,
        scratch_shapes=scratch,
        compiler_params=pltpu.CompilerParams(vmem_limit_bytes=48 * 1024 * 1024),
        cost_estimate=pl.CostEstimate(flops=flops, transcendentals=0,
                                      bytes_accessed=4 * (block_values.size + 3 * rows.size)),
        name="sddp_solve",
    )(block_cols.reshape(-1), rows, vec(inflow), vec(unit_cost), vec(curvature), vec(target),
      vec(release_cap), block_values)


def on_device(trial_states, successor, inflow, unit_cost, curvature, target, release_cap,
              block_values, block_cols):
    states = lax.axis_size("markov")
    tr_rows = trial_states.shape[2]
    width = trial_states.shape[3]
    capacity = 2 * tr_rows // states
    slots = states * capacity
    own_rows = trial_states.reshape(tr_rows, width)
    own_dest = successor.reshape(tr_rows)
    tag = jnp.broadcast_to(own_dest.astype(jnp.float32)[:, None], (tr_rows, BS))
    sent = shifted(jnp.concatenate([own_rows, tag], axis=1), "week", 1)
    rows, dest = sent[:, :width], sent[:, width].astype(jnp.int32)
    marked = (dest[:, None] == jnp.arange(states, dtype=jnp.int32)[None, :]).astype(jnp.int32)
    ranked = jnp.sum(jnp.cumsum(marked, axis=0) * marked, axis=1) - 1
    slot_ids = dest * capacity + ranked
    hit = slot_ids[None, :] == jnp.arange(slots, dtype=jnp.int32)[:, None]
    source = jnp.sum(jnp.where(hit, jnp.arange(tr_rows, dtype=jnp.int32)[None, :], 0), axis=1)
    packed = jnp.take(rows, source.reshape(states, capacity), axis=0, mode="clip")
    arrived = lax.all_to_all(packed, "markov", 0, 0, tiled=True)
    solved = solve_block(arrived.reshape(slots, width), inflow.reshape(width),
                         unit_cost.reshape(width), curvature.reshape(width), target.reshape(width),
                         release_cap.reshape(width), block_values[0, 0], block_cols[0, 0], states)
    back = lax.all_to_all(solved, "markov", 0, 0, tiled=True)
    mine = back.at[dest, ranked].get(mode="clip")
    mine = shifted(mine, "week", -1)
    return (mine[:, :width].reshape(1, 1, tr_rows, width),
            mine[:, width].reshape(1, 1, tr_rows))


def solution(mesh):
    return jax.shard_map(
        on_device,
        mesh=mesh,
        in_specs=(
            P("week", "markov", None, None),
            P("week", "markov", None, None),
            P("week", "markov", None),
            P("week", "markov", None),
            P("week", "markov", None),
            P("week", "markov", None),
            P("week", "markov", None),
            P("week", "markov", None, None, None, None),
            P("week", "markov", None, None),
        ),
        out_specs=(P("week", "markov", None, None), P("week", "markov", None)),
        check_vma=False,
    )
```

```python
import functools

import jax
import jax.numpy as jnp
from jax import lax
from jax.experimental import pallas as pl
from jax.experimental.pallas import tpu as pltpu
from jax.sharding import PartitionSpec as P

ITERS = 4
BS = 128

dual_step = 0.5
primal_step = 0.5


def shifted(value, axis, steps):
    count = lax.axis_size(axis)
    pairs = [(source, (source + steps) % count) for source in range(count)]
    return lax.ppermute(value, axis, pairs)


def dotb(a, b):
    return lax.dot_general(a, b, (((1,), (0,)), ((), ())), preferred_element_type=jnp.float32)


def split(x):
    hi = x.astype(jnp.bfloat16)
    return hi, (x - hi.astype(jnp.float32)).astype(jnp.bfloat16)


def mm(x, wh, wl):
    xh, xl = split(x)
    return dotb(xh, wh) + dotb(xl, wh) + dotb(xh, wl)


def solve_kernel(nblk, kblk, cols_ref, rows_ref, xi_ref, c_ref, q_ref, g_ref, h_ref, bv_ref,
                 out_ref, base_s, p_s, u_s, v_s, acc_s, spread_s, xh_s, xl_s, fh, fl, ah, al):
    width = nblk * BS
    rows_n = rows_ref.shape[0]

    def lanes(n):
        return slice(n * BS, (n + 1) * BS)

    def col(n, k):
        return cols_ref[n * kblk + k]

    for n in range(nblk):
        hi, lo = split(jnp.concatenate([bv_ref[n, k].T for k in range(kblk)], axis=0))
        fh[n] = hi
        fl[n] = lo
        hi, lo = split(jnp.concatenate([bv_ref[n, k] for k in range(kblk)], axis=1))
        ah[n] = hi
        al[n] = lo

    def mixed_fwd(n):
        xh = jnp.concatenate([xh_s[col(n, k)] for k in range(kblk)], axis=1)
        xl = jnp.concatenate([xl_s[col(n, k)] for k in range(kblk)], axis=1)
        return dotb(xh, fh[n]) + dotb(xl, fh[n]) + dotb(xh, fl[n])

    for n in range(nblk):
        s = lanes(n)
        base_s[n] = rows_ref[:, s] + xi_ref[:, s] - g_ref[:, s]
        u_s[n] = jnp.zeros(u_s.shape[1:], jnp.float32)

    for sweep in range(ITERS):
        for n in range(nblk):
            s = lanes(n)
            q = q_ref[:, s]
            shrink = q / (q + dual_step)
            if sweep == 0:
                p_s[n] = (dual_step * base_s[n]) * shrink
            else:
                av = v_s[n] + mixed_fwd(n)
                p_s[n] = (p_s[n] + dual_step * (base_s[n] - av)) * shrink
        for n in range(nblk):
            spread_s[n] = mm(p_s[n], ah[n], al[n])
        for n in range(nblk):
            acc_s[n] = p_s[n]
        for n in range(nblk):
            for k in range(kblk):
                c = col(n, k)
                acc_s[c] = acc_s[c] + spread_s[n, :, k * BS:(k + 1) * BS]
        for n in range(nblk):
            s = lanes(n)
            u_old = u_s[n]
            fresh = jnp.clip(u_old + primal_step * (acc_s[n] - c_ref[:, s]), 0.0, h_ref[:, s])
            v = 2.0 * fresh - u_old
            v_s[n] = v
            u_s[n] = fresh
            hi, lo = split(fresh if sweep == ITERS - 1 else v)
            xh_s[n] = hi
            xl_s[n] = lo

    value = jnp.zeros((rows_n, BS), jnp.float32)
    cross = jnp.zeros((rows_n, BS), jnp.float32)
    for n in range(nblk):
        s = lanes(n)
        rows = rows_ref[:, s]
        un = u_s[n]
        gap = rows + xi_ref[:, s] - (un + mixed_fwd(n)) - g_ref[:, s]
        value = value + (c_ref[:, s] * un + 0.5 * q_ref[:, s] * gap * gap)
        pn = p_s[n]
        cross = cross + pn * rows
        out_ref[:, :, s] = pn.reshape(out_ref.shape[0], out_ref.shape[1], BS)
    icpt = (jnp.sum(value, axis=1, keepdims=True) - jnp.sum(cross, axis=1, keepdims=True)) / width
    out_ref[:, :, width:] = jnp.broadcast_to(icpt, (rows_n, BS)).reshape(out_ref.shape[0], out_ref.shape[1], BS)


def solve_block(rows, inflow, unit_cost, curvature, target, release_cap, block_values, block_cols,
                groups):
    count, width = rows.shape
    nblk, kblk = block_values.shape[0], block_values.shape[1]
    vec = lambda a: a.reshape(1, width)
    vspec = pl.BlockSpec(memory_space=pltpu.VMEM)
    field = pltpu.VMEM((nblk, count, BS), jnp.float32)
    scratch = [field] * 5 + [pltpu.VMEM((nblk, count, kblk * BS), jnp.float32)]
    scratch += [pltpu.VMEM((nblk, count, BS), jnp.bfloat16)] * 2
    scratch += [pltpu.VMEM((nblk, kblk * BS, BS), jnp.bfloat16)] * 2
    scratch += [pltpu.VMEM((nblk, BS, kblk * BS), jnp.bfloat16)] * 2
    flops = 2 * count * nblk * kblk * BS * BS * (2 * ITERS) * 3
    return pl.pallas_call(
        functools.partial(solve_kernel, nblk, kblk),
        out_shape=jax.ShapeDtypeStruct((groups, count // groups, width + BS), jnp.float32),
        in_specs=[pl.BlockSpec(memory_space=pltpu.SMEM)] + [vspec] * 7,
        out_specs=vspec,
        scratch_shapes=scratch,
        compiler_params=pltpu.CompilerParams(vmem_limit_bytes=48 * 1024 * 1024),
        cost_estimate=pl.CostEstimate(flops=flops, transcendentals=0,
                                      bytes_accessed=4 * (block_values.size + 3 * rows.size)),
        name="sddp_solve",
    )(block_cols.reshape(-1), rows, vec(inflow), vec(unit_cost), vec(curvature), vec(target),
      vec(release_cap), block_values)


def on_device(trial_states, successor, inflow, unit_cost, curvature, target, release_cap,
              block_values, block_cols):
    states = lax.axis_size("markov")
    tr_rows = trial_states.shape[2]
    width = trial_states.shape[3]
    capacity = 2 * tr_rows // states
    slots = states * capacity
    own_rows = trial_states.reshape(tr_rows, width)
    own_dest = successor.reshape(tr_rows)
    tag = jnp.broadcast_to(own_dest.astype(jnp.float32)[:, None], (tr_rows, BS))
    sent = shifted(jnp.concatenate([own_rows, tag], axis=1), "week", 1)
    rows, dest = sent[:, :width], sent[:, width].astype(jnp.int32)
    marked = (dest[:, None] == jnp.arange(states, dtype=jnp.int32)[None, :]).astype(jnp.int32)
    ranked = jnp.sum(jnp.cumsum(marked, axis=0) * marked, axis=1) - 1
    slot_ids = dest * capacity + ranked
    hit = slot_ids[None, :] == jnp.arange(slots, dtype=jnp.int32)[:, None]
    source = jnp.sum(jnp.where(hit, jnp.arange(tr_rows, dtype=jnp.int32)[None, :], 0), axis=1)
    packed = jnp.take(rows, source.reshape(states, capacity), axis=0, mode="clip")
    arrived = lax.all_to_all(packed, "markov", 0, 0, tiled=True)
    solved = solve_block(arrived.reshape(slots, width), inflow.reshape(width),
                         unit_cost.reshape(width), curvature.reshape(width), target.reshape(width),
                         release_cap.reshape(width), block_values[0, 0], block_cols[0, 0], states)
    back = lax.all_to_all(solved, "markov", 0, 0, tiled=True)
    mine = back.at[dest, ranked].get(mode="clip")
    mine = shifted(mine, "week", -1)
    return (mine[:, :width].reshape(1, 1, tr_rows, width),
            mine[:, width].reshape(1, 1, tr_rows))


def solution(mesh):
    return jax.shard_map(
        on_device,
        mesh=mesh,
        in_specs=(
            P("week", "markov", None, None),
            P("week", "markov", None, None),
            P("week", "markov", None),
            P("week", "markov", None),
            P("week", "markov", None),
            P("week", "markov", None),
            P("week", "markov", None),
            P("week", "markov", None, None, None, None),
            P("week", "markov", None, None),
        ),
        out_specs=(P("week", "markov", None, None), P("week", "markov", None)),
        check_vma=False,
    )
```

```python
import functools

import jax
import jax.numpy as jnp
from jax import lax
from jax.experimental import pallas as pl
from jax.experimental.pallas import tpu as pltpu
from jax.sharding import PartitionSpec as P

ITERS = 4
BS = 128

dual_step = 0.5
primal_step = 0.5


def shifted(value, axis, steps):
    count = lax.axis_size(axis)
    pairs = [(source, (source + steps) % count) for source in range(count)]
    return lax.ppermute(value, axis, pairs)


def dotb(a, b):
    return lax.dot_general(a, b, (((1,), (0,)), ((), ())), preferred_element_type=jnp.float32)


def split(x):
    hi = x.astype(jnp.bfloat16)
    return hi, (x - hi.astype(jnp.float32)).astype(jnp.bfloat16)


def mm(x, wh, wl):
    xh, xl = split(x)
    return dotb(xh, wh) + dotb(xl, wh) + dotb(xh, wl)


def solve_kernel(nblk, kblk, cols_ref, rows_ref, xi_ref, c_ref, q_ref, g_ref, h_ref, bv_ref,
                 out_ref, base_s, p_s, u_s, v_s, acc_s, spread_s, shrink_s, fh, fl, ah, al):
    width = nblk * BS
    rows_n = rows_ref.shape[0]

    def lanes(n):
        return slice(n * BS, (n + 1) * BS)

    def col(n, k):
        return cols_ref[n * kblk + k]

    for n in range(nblk):
        hi, lo = split(jnp.concatenate([bv_ref[n, k].T for k in range(kblk)], axis=0))
        fh[n] = hi
        fl[n] = lo
        hi, lo = split(jnp.concatenate([bv_ref[n, k] for k in range(kblk)], axis=1))
        ah[n] = hi
        al[n] = lo

    def mixed_fwd(field_s, n):
        x = jnp.concatenate([field_s[col(n, k)] for k in range(kblk)], axis=1)
        return mm(x, fh[n], fl[n])

    for n in range(nblk):
        s = lanes(n)
        base_s[n] = rows_ref[:, s] + xi_ref[:, s] - g_ref[:, s]
        u_s[n] = jnp.zeros(u_s.shape[1:], jnp.float32)

    for n in range(nblk):
        q = q_ref[:, lanes(n)]
        shrink_s[n] = q / (q + dual_step)

    for sweep in range(ITERS):
        for n in range(nblk):
            shrink = shrink_s[n]
            if sweep == 0:
                p_s[n] = (dual_step * base_s[n]) * shrink
            else:
                av = v_s[n] + mixed_fwd(v_s, n)
                p_s[n] = (p_s[n] + dual_step * (base_s[n] - av)) * shrink
        for n in range(nblk):
            spread_s[n] = mm(p_s[n], ah[n], al[n])
        for n in range(nblk):
            acc_s[n] = p_s[n]
        for n in range(nblk):
            for k in range(kblk):
                c = col(n, k)
                acc_s[c] = acc_s[c] + spread_s[n, :, k * BS:(k + 1) * BS]
        for n in range(nblk):
            s = lanes(n)
            u_old = u_s[n]
            fresh = jnp.clip(u_old + primal_step * (acc_s[n] - c_ref[:, s]), 0.0, h_ref[:, s])
            v_s[n] = 2.0 * fresh - u_old
            u_s[n] = fresh

    value = jnp.zeros((rows_n, BS), jnp.float32)
    cross = jnp.zeros((rows_n, BS), jnp.float32)
    for n in range(nblk):
        s = lanes(n)
        rows = rows_ref[:, s]
        un = u_s[n]
        gap = rows + xi_ref[:, s] - (un + mixed_fwd(u_s, n)) - g_ref[:, s]
        value = value + (c_ref[:, s] * un + 0.5 * q_ref[:, s] * gap * gap)
        pn = p_s[n]
        cross = cross + pn * rows
        out_ref[:, :, s] = pn.reshape(out_ref.shape[0], out_ref.shape[1], BS)
    icpt = (jnp.sum(value, axis=1, keepdims=True) - jnp.sum(cross, axis=1, keepdims=True)) / width
    out_ref[:, :, width:] = jnp.broadcast_to(icpt, (rows_n, BS)).reshape(out_ref.shape[0], out_ref.shape[1], BS)


def solve_block(rows, inflow, unit_cost, curvature, target, release_cap, block_values, block_cols,
                groups):
    count, width = rows.shape
    nblk, kblk = block_values.shape[0], block_values.shape[1]
    vec = lambda a: a.reshape(1, width)
    vspec = pl.BlockSpec(memory_space=pltpu.VMEM)
    field = pltpu.VMEM((nblk, count, BS), jnp.float32)
    scratch = [field] * 5 + [pltpu.VMEM((nblk, count, kblk * BS), jnp.float32)]
    scratch += [pltpu.VMEM((nblk, 1, BS), jnp.float32)]
    scratch += [pltpu.VMEM((nblk, kblk * BS, BS), jnp.bfloat16)] * 2
    scratch += [pltpu.VMEM((nblk, BS, kblk * BS), jnp.bfloat16)] * 2
    flops = 2 * count * nblk * kblk * BS * BS * (2 * ITERS) * 3
    return pl.pallas_call(
        functools.partial(solve_kernel, nblk, kblk),
        out_shape=jax.ShapeDtypeStruct((groups, count // groups, width + BS), jnp.float32),
        in_specs=[pl.BlockSpec(memory_space=pltpu.SMEM)] + [vspec] * 7,
        out_specs=vspec,
        scratch_shapes=scratch,
        compiler_params=pltpu.CompilerParams(vmem_limit_bytes=48 * 1024 * 1024),
        cost_estimate=pl.CostEstimate(flops=flops, transcendentals=0,
                                      bytes_accessed=4 * (block_values.size + 3 * rows.size)),
        name="sddp_solve",
    )(block_cols.reshape(-1), rows, vec(inflow), vec(unit_cost), vec(curvature), vec(target),
      vec(release_cap), block_values)


def on_device(trial_states, successor, inflow, unit_cost, curvature, target, release_cap,
              block_values, block_cols):
    states = lax.axis_size("markov")
    tr_rows = trial_states.shape[2]
    width = trial_states.shape[3]
    capacity = 2 * tr_rows // states
    slots = states * capacity
    own_rows = trial_states.reshape(tr_rows, width)
    own_dest = successor.reshape(tr_rows)
    tag = jnp.broadcast_to(own_dest.astype(jnp.float32)[:, None], (tr_rows, BS))
    sent = shifted(jnp.concatenate([own_rows, tag], axis=1), "week", 1)
    rows, dest = sent[:, :width], sent[:, width].astype(jnp.int32)
    marked = (dest[:, None] == jnp.arange(states, dtype=jnp.int32)[None, :]).astype(jnp.int32)
    ranked = jnp.sum(jnp.cumsum(marked, axis=0) * marked, axis=1) - 1
    slot_ids = dest * capacity + ranked
    hit = slot_ids[None, :] == jnp.arange(slots, dtype=jnp.int32)[:, None]
    source = jnp.sum(jnp.where(hit, jnp.arange(tr_rows, dtype=jnp.int32)[None, :], 0), axis=1)
    packed = jnp.take(rows, source.reshape(states, capacity), axis=0, mode="clip")
    arrived = lax.all_to_all(packed, "markov", 0, 0, tiled=True)
    solved = solve_block(arrived.reshape(slots, width), inflow.reshape(width),
                         unit_cost.reshape(width), curvature.reshape(width), target.reshape(width),
                         release_cap.reshape(width), block_values[0, 0], block_cols[0, 0], states)
    back = lax.all_to_all(solved, "markov", 0, 0, tiled=True)
    mine = back.at[dest, ranked].get(mode="clip")
    mine = shifted(mine, "week", -1)
    return (mine[:, :width].reshape(1, 1, tr_rows, width),
            mine[:, width].reshape(1, 1, tr_rows))


def solution(mesh):
    return jax.shard_map(
        on_device,
        mesh=mesh,
        in_specs=(
            P("week", "markov", None, None),
            P("week", "markov", None, None),
            P("week", "markov", None),
            P("week", "markov", None),
            P("week", "markov", None),
            P("week", "markov", None),
            P("week", "markov", None),
            P("week", "markov", None, None, None, None),
            P("week", "markov", None, None),
        ),
        out_specs=(P("week", "markov", None, None), P("week", "markov", None)),
        check_vma=False,
    )
```
